512 devices in a mesh: lat: 32 (over y, x_hi, core), lon: 16 (over z, x_lo).
Axes of the slice: x: 4 (x_hi: 2, x_lo: 2; x = x_hi * 2 + x_lo), y: 8, z: 8, core: 2. Of those that a mesh axis runs over, the one named last changes fastest.
Arguments:
- tracers: float32 [5, 1, 3072, 2048], P(None, None, 'lat', 'lon'), may hold values from 0.2 to 2
- offsets: int32 [3072, 2048], P('lat', 'lon'), may hold values from 0 to 255, as said below
- fraction: float32 [3072, 2048], P('lat', 'lon'), may hold values from 0 to 0.95
- courant_north: float32 [3072, 2048], P('lat', 'lon'), may hold values from 0 to 0.9
Outputs:
- advected: float32 [5, 1, 3072, 2048], P(None, None, 'lat', 'lon')
The draws below stay inside these ranges and needn't reach their ends.
Inputs may be any that keep to these rules, and one draw needn't show every extreme that they name: Let k = min(r, 3071 - r) for row r. Rows with k < 24 have offsets from 128 to 255, the largest reached in row 0; rows with 24 <= k < 48 have offsets at most 64, reached in row 24; all other rows have offsets at most 8, reached in row 48. Offsets of adjacent faces g and g + 1 of a row differ by at most one.
All inputs are finite; a program needn't handle non-finite values.
Results may differ from the reference program's by a relative error of at most 0.0003.
Values sent between devices are 32-bit elements; how exact they have to be, the bound alone decides.
A program may use at most 64 MiB of HBM per device.

```python
import jax
import jax.numpy as jnp
from jax import lax

NTR = 5
LEV = 1
LON_DEV = 128
MID = 8
REACH = 64
POLAR = 24
NLAT = 3072
NLON = 2048


def draw_offsets(key, part):
    key_start = jax.random.fold_in(key, 21)
    key_step = jax.random.fold_in(key, 22)
    row_index = jnp.arange(NLAT, dtype=jnp.int32)
    pole_distance = jnp.minimum(row_index, NLAT - 1 - row_index)
    polar_rows = pole_distance < POLAR
    band_rows = (pole_distance >= POLAR) & (pole_distance < 2 * POLAR)
    lowest = jnp.where(polar_rows, LON_DEV, 0).astype(jnp.int32)
    highest = jnp.where(polar_rows, 2 * LON_DEV - 1, jnp.where(band_rows, REACH, MID)).astype(jnp.int32)
    raw_start = jax.random.randint(key_start, (NLAT,), 0, 1 << 20, dtype=jnp.int32)
    row_start = (lowest + raw_start % (highest - lowest + 1)).astype(jnp.int32)
    row_start = jnp.where(row_index == 0, 2 * LON_DEV - 1, row_start)
    row_start = jnp.where(row_index == POLAR, REACH, row_start)
    row_start = jnp.where(row_index == 2 * POLAR, MID, row_start).astype(jnp.int32)
    steps_taken = jax.random.randint(key_step, (NLAT, NLON), -1, 2, dtype=jnp.int32)
    walk_value = (row_start[:, None] + jnp.cumsum(steps_taken, axis=1) - steps_taken[:, 0:1]).astype(jnp.int32)
    return jnp.clip(walk_value, lowest[:, None], highest[:, None]).astype(jnp.int32)


def level_of(rng, dims, cuts, least, top_value):
    level = 1.0
    for position, shards_of in cuts:
        steps = jax.random.uniform(jax.random.fold_in(jax.random.fold_in(rng, 6), position), (shards_of,), jnp.float32, least / len(cuts), top_value / len(cuts))
        level = level * jnp.repeat(jnp.exp(steps), dims[position] // shards_of).reshape((-1,) + (1,) * (len(dims) - 1 - position))
    return level


def setup_inputs(seed: int = 0) -> dict:
    splits = jax.random.split(jax.random.key(seed), 5)
    return {
        "tracers": jnp.clip(0.2 + 1.8 * jax.random.uniform(splits[0], (NTR, LEV, NLAT, NLON), jnp.float32) ** level_of(splits[0], (NTR, LEV, NLAT, NLON), ((2, 32), (3, 16)), -0.2, 0.2), 0.2, 2.0),
        "offsets": draw_offsets(jax.random.fold_in(splits[4], 71), 0),
        "fraction": jnp.clip(0.95 * jax.random.uniform(splits[2], (NLAT, NLON), jnp.float32) ** level_of(splits[2], (NLAT, NLON), ((0, 32), (1, 16)), -0.2, 0.2), 0.0, 0.95),
        "courant_north": jnp.clip(0.9 * jax.random.uniform(splits[3], (NLAT, NLON), jnp.float32) ** level_of(splits[3], (NLAT, NLON), ((0, 32), (1, 16)), -0.2, 0.2), 0.0, 0.9),
    }


wide_weight = 7.0 / 12.0
narrow_weight = 1.0 / 12.0


def frac_flux(courant, right_edge, edge_jump, curvature):
    return courant * (right_edge - 0.5 * courant * (edge_jump - (1.0 - (2.0 / 3.0) * courant) * curvature))


def reference(tracers, offsets, fraction, courant_north):
    blocks = NLON // LON_DEV
    face_index = jnp.arange(NLON, dtype=jnp.int32)
    block_own = face_index // LON_DEV
    start_cell = face_index[None, :] - offsets
    block_src = jnp.floor_divide(start_cell, LON_DEV)
    distance = block_own[None, :] - block_src
    first_mask = (distance >= 1).astype(jnp.float32)
    second_mask = (distance >= 2).astype(jnp.float32)
    start_wrapped = jnp.mod(start_cell, NLON).astype(jnp.int32)
    depart_cell = jnp.mod(start_cell - 1, NLON).astype(jnp.int32)
    prev_one = jnp.mod(block_own - 1, blocks).astype(jnp.int32)
    prev_two = jnp.mod(block_own - 2, blocks).astype(jnp.int32)
    later = lax.broadcasted_iota(jnp.int32, (LON_DEV, LON_DEV), 1)
    earlier = lax.broadcasted_iota(jnp.int32, (LON_DEV, LON_DEV), 0)
    strictly_before = (earlier < later).astype(jnp.float32)
    courant = jnp.concatenate([jnp.zeros((1, NLON), jnp.float32), courant_north[1:], jnp.zeros((1, NLON), jnp.float32)], axis=0)

    def one_slice(field):
        left_edge = wide_weight * (jnp.roll(field, 1, 1) + field) - narrow_weight * (jnp.roll(field, 2, 1) + jnp.roll(field, -1, 1))
        right_edge = wide_weight * (field + jnp.roll(field, -1, 1)) - narrow_weight * (jnp.roll(field, 1, 1) + jnp.roll(field, -2, 1))
        edge_jump = right_edge - left_edge
        curvature = 6.0 * (field - 0.5 * (left_edge + right_edge))
        grouped = field.reshape(NLAT, blocks, LON_DEV)
        prefix = jnp.dot(grouped, strictly_before, precision=lax.Precision.HIGHEST).reshape(NLAT, NLON)
        block_total = jnp.sum(grouped, axis=2)
        total_one = jnp.take(block_total, prev_one, axis=1)
        total_two = jnp.take(block_total, prev_two, axis=1)
        base_value = jnp.take_along_axis(prefix, start_wrapped, axis=1) - (total_one * first_mask + total_two * second_mask)
        part_right = jnp.take_along_axis(right_edge, depart_cell, axis=1)
        part_jump = jnp.take_along_axis(edge_jump, depart_cell, axis=1)
        part_curve = jnp.take_along_axis(curvature, depart_cell, axis=1)
        zonal_flux = (prefix - base_value) + frac_flux(fraction, part_right, part_jump, part_curve)
        after_zonal = field - (jnp.roll(zonal_flux, -1, 1) - zonal_flux)
        padded = jnp.pad(after_zonal, ((3, 3), (0, 0)))

        def row_window(shift_by):
            return padded[2 + shift_by:3 + shift_by + NLAT]

        merid_left = wide_weight * (row_window(-1) + row_window(0)) - narrow_weight * (row_window(-2) + row_window(1))
        merid_right = wide_weight * (row_window(0) + row_window(1)) - narrow_weight * (row_window(-1) + row_window(2))
        merid_jump = merid_right - merid_left
        merid_curve = 6.0 * (row_window(0) - 0.5 * (merid_left + merid_right))
        merid_flux = frac_flux(courant, merid_right, merid_jump, merid_curve)
        return after_zonal - (merid_flux[1:] - merid_flux[:-1])

    stacked = tracers.reshape(NTR * LEV, NLAT, NLON)
    result = lax.map(one_slice, stacked)
    return result.reshape(NTR, LEV, NLAT, NLON)
```

```python
import functools

import jax
import jax.numpy as jnp
from jax import lax
from jax.experimental import pallas as pl
from jax.experimental.pallas import tpu as pltpu
from jax.sharding import PartitionSpec as P

wide_weight = 7.0 / 12.0
narrow_weight = 1.0 / 12.0
MESH = pl.DeviceIdType.MESH
SUB = 8
RIM = 16
POLAR_GROUPS = 3
FULL_GROUPS = 6


def take(table, index):
    return jnp.take_along_axis(table, index, axis=1, mode="promise_in_bounds")


def split_dot(value, matrix):
    high = value.astype(jnp.bfloat16)
    low = (value - high.astype(jnp.float32)).astype(jnp.bfloat16)
    return jnp.dot(high, matrix, preferred_element_type=jnp.float32) + jnp.dot(
        low, matrix, preferred_element_type=jnp.float32
    )


def frac_flux(courant, right, left, centre):
    jump = right - left
    curve = 6.0 * (centre - 0.5 * (left + right))
    return courant * (right - 0.5 * courant * (jump - (1.0 - 2.0 / 3.0 * courant) * curve))


def roll(value, steps):
    steps = steps % value.shape[-1]
    return value if steps == 0 else pltpu.roll(value, steps, 1)


def edge_pair(cells, west, east, lane):
    last = cells.shape[-1]
    minus_two = roll(jnp.where(lane >= last - 2, west, cells), 2)
    minus_one = roll(jnp.where(lane >= last - 1, west, cells), 1)
    plus_one = roll(jnp.where(lane < 1, east, cells), -1)
    plus_two = roll(jnp.where(lane < 2, east, cells), -2)
    left = wide_weight * (minus_one + cells) - narrow_weight * (minus_two + plus_one)
    right = wide_weight * (cells + plus_one) - narrow_weight * (minus_one + plus_two)
    return left, right


def kernel(
    sizes, tr, off_in, fr_in, cn_in, out,
    buf, off_buf, fr_buf, cn_buf, west_two, pack, ecol, got_pack, got_ecol, got_far,
    lo_buf, prefix, total, suffix, after, edge_buf, flux_buf,
    local_sem, send_sem, recv_sem,
):
    lat_count, lon_count = sizes
    depth, rows, lanes = tr.shape
    groups = rows // SUB
    slots = lanes // RIM
    lat, lon = lax.axis_index("lat"), lax.axis_index("lon")
    south_end = lat == 0
    north_end = lat == lat_count - 1
    polar = south_end | north_end

    local = [
        pltpu.make_async_copy(tr, buf.at[0], local_sem.at[0]),
        pltpu.make_async_copy(off_in, off_buf, local_sem.at[1]),
        pltpu.make_async_copy(fr_in, fr_buf, local_sem.at[2]),
        pltpu.make_async_copy(cn_in, cn_buf.at[pl.ds(0, rows)], local_sem.at[3]),
    ]
    for copy in local:
        copy.start()

    def lon_dev(steps):
        return {"lat": lat, "lon": lax.rem(lon + steps + lon_count, lon_count)}

    def lat_dev(steps):
        return {"lat": lax.rem(lat + steps + lat_count, lat_count), "lon": lon}

    barrier = pltpu.get_barrier_semaphore()
    for device in (lon_dev(1), lon_dev(-1), lat_dev(1), lat_dev(-1)):
        pl.semaphore_signal(barrier, inc=1, device_id=device, device_id_type=MESH)

    @pl.when(polar)
    def _():
        for steps in (2, -2, 3, -3):
            pl.semaphore_signal(barrier, inc=1, device_id=lon_dev(steps), device_id_type=MESH)

    lane = lax.broadcasted_iota(jnp.int32, (SUB, lanes), 1)
    slot_of = lane // RIM

    for copy in local[:3]:
        copy.wait()

    for tile in range(-(-depth * groups // slots)):
        packed = jnp.zeros((SUB, lanes), jnp.float32)
        for slot in range(slots):
            group, t = divmod(tile * slots + slot, depth)
            if group >= groups:
                break
            cells = buf[0, t, group * SUB : (group + 1) * SUB, :]
            packed = jnp.where(slot_of == slot, roll(cells, RIM * (slot + 1)), packed)
        pack[tile] = packed
    for tile in range(ecol.shape[0]):
        packed = jnp.zeros((SUB, lanes), jnp.float32)
        for slot in range(slots):
            group = tile * slots + slot
            if group >= groups:
                break
            span = slice(group * SUB, (group + 1) * SUB)
            base = slot * RIM
            for t in range(depth):
                at = base + 2 * t
                packed = jnp.where((lane >= at) & (lane < at + 2), roll(buf[0, t, span, :], at), packed)
            at = base + 2 * depth
            packed = jnp.where(lane == at, roll(off_buf[span, :].astype(jnp.float32), at), packed)
            packed = jnp.where(lane == at + 1, roll(fr_buf[span, :], at + 1), packed)
        ecol[tile] = packed

    pl.semaphore_wait(barrier, jnp.where(polar, 8, 4))

    def remote(source, target, index, device):
        return pltpu.make_async_remote_copy(
            src_ref=source, dst_ref=target, send_sem=send_sem.at[index], recv_sem=recv_sem.at[index],
            device_id=device, device_id_type=MESH,
        )

    full_row = jnp.where(south_end, 0, rows - FULL_GROUPS * SUB)
    full_span = pl.ds(pl.multiple_of(full_row, SUB), FULL_GROUPS * SUB)
    polar_row = jnp.where(south_end, 0, rows - POLAR_GROUPS * SUB)
    polar_span = pl.ds(pl.multiple_of(polar_row, SUB), POLAR_GROUPS * SUB)
    far_span = pl.ds(jnp.where(south_end, 0, pack.shape[0] - 3), 3)
    polar_copies = [
        remote(tr.at[:, full_span], buf.at[1, :, full_span], 3, lon_dev(1)),
        remote(tr.at[:, polar_span], west_two.at[:, polar_span], 4, lon_dev(2)),
        remote(pack.at[far_span], got_far.at[far_span], 5, lon_dev(3)),
    ]

    @pl.when(polar)
    def _():
        for copy in polar_copies:
            copy.start()

    rim_copies = [
        remote(pack, got_pack, 0, lon_dev(1)),
        remote(ecol, got_ecol, 1, lon_dev(-1)),
        remote(cn_in.at[pl.ds(0, SUB)], cn_buf.at[pl.ds(rows, SUB)], 2, lat_dev(-1)),
    ]
    for copy in rim_copies:
        copy.start()

    row_of = lax.broadcasted_iota(jnp.int32, (lanes, lanes), 0)
    col_of = lax.broadcasted_iota(jnp.int32, (lanes, lanes), 1)
    ones = jnp.ones((lanes, lanes), jnp.float32)
    upto = (row_of <= col_of).astype(jnp.float32)
    prefix_matrix = jnp.concatenate([upto, ones], axis=1).astype(jnp.bfloat16)
    suffix_matrix = (upto - ones).astype(jnp.bfloat16)

    def prefix_of(which, t):
        both = split_dot(buf[which, t], prefix_matrix)
        prefix[which, t] = both[:, :lanes]
        total[which, t] = both[:, lanes:]

    for t in range(depth):
        prefix_of(0, t)
    local[3].wait()

    for copy in rim_copies[:2]:
        copy.wait()

    @pl.when(polar)
    def _():
        for copy in polar_copies:
            copy.wait()
        for t in range(depth):
            prefix_of(1, t)

    def is_polar(group):
        return (south_end & (group < POLAR_GROUPS)) | (north_end & (group >= groups - POLAR_GROUPS))

    def is_full(group):
        return (south_end & (group < FULL_GROUPS)) | (north_end & (group >= groups - FULL_GROUPS))

    for tile in range(-(-depth * groups // slots)):
        packed = got_pack[tile]
        for slot in range(slots):
            group, t = divmod(tile * slots + slot, depth)
            if group >= groups:
                break
            span = slice(group * SUB, (group + 1) * SUB)
            lo_buf[t, span, :] = jnp.where(lane >= lanes - RIM, roll(packed, -RIM * (slot + 1)), 0.0)

    @pl.when(polar)
    def _():
        lo_buf[:, full_span, :] = buf[1, :, full_span, :]
        lo_buf[:, polar_span, :] = west_two[:, polar_span, :]

    for t in range(depth):
        suffix[t] = split_dot(lo_buf[t], suffix_matrix)

    def zonal(group):
        first = pl.multiple_of(group * SUB, SUB)
        span = pl.ds(first, SUB)
        far = jnp.where(is_polar(group), 1, 0)
        off = off_buf[span, :]
        courant = fr_buf[span, :]
        east = got_ecol[group // slots]
        base = lax.rem(group, slots) * RIM
        east_off = take(east, jnp.full((SUB, lanes), 0, jnp.int32) + (base + 2 * depth)).astype(jnp.int32)
        east_courant = take(east, jnp.full((SUB, lanes), 0, jnp.int32) + (base + 2 * depth + 1))
        depart = lane - off - 1 + far * lanes
        in_lo = depart < 0
        index = depart & (lanes - 1)
        east_index = (lanes - 1 - east_off + far * lanes) & (lanes - 1)
        for t in range(depth):
            own = buf[0, t, span, :]
            near = buf[far, t, span, :]
            low = lo_buf[t, span, :]
            order = group * depth + t
            beyond = take(got_far[order // slots], (lane + RIM * (lax.rem(order, slots) + 1)) & (lanes - 1))
            ahead = take(east, (lane + (base + 2 * t)) & (lanes - 1))
            ahead = jnp.where(far == 1, own, ahead)
            near_left, near_right = edge_pair(near, low, ahead, lane)
            low_left, low_right = edge_pair(low, beyond, near, lane)
            near_prefix = prefix[far, t, span, :]
            far_total = jnp.where(far == 1, total[far, t, span, :], 0.0)

            def pick(near_table, low_table):
                return jnp.where(in_lo, take(low_table, index), take(near_table, index))

            flux = (
                (prefix[0, t, span, :] - own + far_total)
                - pick(near_prefix, suffix[t, span, :])
                + frac_flux(courant, pick(near_right, low_right), pick(near_left, low_left), pick(near, low))
            )
            east_flux = (
                (total[0, t, span, :] + far_total)
                - take(near_prefix, east_index)
                + frac_flux(
                    east_courant, take(near_right, east_index), take(near_left, east_index), take(near, east_index)
                )
            )
            next_flux = roll(jnp.where(lane == 0, east_flux, flux), -1)
            after[t, pl.ds(pl.multiple_of(first + SUB, SUB), SUB), :] = own - (next_flux - flux)

    def edge_group(i, carry):
        zonal(i * (groups - 1))
        return carry

    lax.fori_loop(0, 2, edge_group, 0)
    lat_copies = [
        remote(after.at[:, pl.ds(SUB, SUB)], after.at[:, pl.ds(SUB + rows, SUB)], 6, lat_dev(-1)),
        remote(after.at[:, pl.ds(rows, SUB)], after.at[:, pl.ds(0, SUB)], 7, lat_dev(1)),
    ]
    for copy in lat_copies:
        copy.start()

    def inner_group(i, carry):
        zonal(i)
        return carry

    lax.fori_loop(1, groups - 1, inner_group, 0)
    rim_copies[2].wait()
    for copy in lat_copies:
        copy.wait()

    @pl.when(south_end)
    def _():
        after[:, 0:SUB, :] = jnp.zeros((depth, SUB, lanes), jnp.float32)
        cn_buf[0:1, :] = jnp.zeros((1, lanes), jnp.float32)

    @pl.when(north_end)
    def _():
        after[:, SUB + rows :, :] = jnp.zeros((depth, SUB, lanes), jnp.float32)
        cn_buf[rows:, :] = jnp.zeros((SUB, lanes), jnp.float32)

    courant = cn_buf[0 : rows + 1, :]
    for t in range(depth):
        edge_buf[t, 0 : rows + 2, :] = wide_weight * (
            after[t, SUB - 2 : SUB + rows, :] + after[t, SUB - 1 : SUB + rows + 1, :]
        ) - narrow_weight * (after[t, SUB - 3 : SUB + rows - 1, :] + after[t, SUB : SUB + rows + 2, :])
        flux_buf[t, 0 : rows + 1, :] = frac_flux(
            courant,
            edge_buf[t, 1 : rows + 2, :],
            edge_buf[t, 0 : rows + 1, :],
            after[t, SUB - 1 : SUB + rows, :],
        )
        out[t] = after[t, SUB : SUB + rows, :] - (flux_buf[t, 1 : rows + 1, :] - flux_buf[t, 0:rows, :])


def on_device(sizes, tracers, offsets, fraction, courant_north):
    tracer_count, level_count, rows, lanes = tracers.shape
    depth = tracer_count * level_count
    f32 = jnp.float32
    groups = rows // SUB
    slots = lanes // RIM
    advected = pl.pallas_call(
        functools.partial(kernel, sizes),
        out_shape=jax.ShapeDtypeStruct((depth, rows, lanes), f32),
        in_specs=[pl.BlockSpec(memory_space=pl.ANY)] * 4,
        out_specs=pl.BlockSpec(memory_space=pltpu.VMEM),
        scratch_shapes=[
            pltpu.VMEM((2, depth, rows, lanes), f32),
            pltpu.VMEM((rows, lanes), jnp.int32),
            pltpu.VMEM((rows, lanes), f32),
            pltpu.VMEM((rows + SUB, lanes), f32),
            pltpu.VMEM((depth, rows, lanes), f32),
            pltpu.VMEM((-(-depth * groups // slots), SUB, lanes), f32),
            pltpu.VMEM((-(-groups // slots), SUB, lanes), f32),
            pltpu.VMEM((-(-depth * groups // slots), SUB, lanes), f32),
            pltpu.VMEM((-(-groups // slots), SUB, lanes), f32),
            pltpu.VMEM((-(-depth * groups // slots), SUB, lanes), f32),
            pltpu.VMEM((depth, rows, lanes), f32),
            pltpu.VMEM((2, depth, rows, lanes), f32),
            pltpu.VMEM((2, depth, rows, lanes), f32),
            pltpu.VMEM((depth, rows, lanes), f32),
            pltpu.VMEM((depth, rows + 2 * SUB, lanes), f32),
            pltpu.VMEM((depth, rows + SUB, lanes), f32),
            pltpu.VMEM((depth, rows + SUB, lanes), f32),
            pltpu.SemaphoreType.DMA((4,)),
            pltpu.SemaphoreType.DMA((8,)),
            pltpu.SemaphoreType.DMA((8,)),
        ],
        compiler_params=pltpu.CompilerParams(collective_id=0, has_side_effects=True),
    )(tracers.reshape(depth, rows, lanes), offsets, fraction, courant_north)
    return advected.reshape(tracers.shape)


def solution(mesh):
    placed = (P(None, None, "lat", "lon"), P("lat", "lon"), P("lat", "lon"), P("lat", "lon"))
    return jax.shard_map(
        functools.partial(on_device, (mesh.shape["lat"], mesh.shape["lon"])),
        mesh=mesh,
        in_specs=placed,
        out_specs=P(None, None, "lat", "lon"),
        check_vma=False,
    )
```

```python
import functools

import jax
import jax.numpy as jnp
from jax import lax
from jax.experimental import pallas as pl
from jax.experimental.pallas import tpu as pltpu
from jax.sharding import PartitionSpec as P

wide_weight = 7.0 / 12.0
narrow_weight = 1.0 / 12.0
MESH = pl.DeviceIdType.MESH
SUB = 8
RIM = 16
POLAR_GROUPS = 3
FULL_GROUPS = 6


def take(table, index):
    return jnp.take_along_axis(table, index, axis=1, mode="promise_in_bounds")


def split_dot(value, matrix):
    high = value.astype(jnp.bfloat16)
    low = (value - high.astype(jnp.float32)).astype(jnp.bfloat16)
    return jnp.dot(high, matrix, preferred_element_type=jnp.float32) + jnp.dot(
        low, matrix, preferred_element_type=jnp.float32
    )


def frac_flux(courant, right, left, centre):
    jump = right - left
    curve = 6.0 * (centre - 0.5 * (left + right))
    return courant * (right - 0.5 * courant * (jump - (1.0 - 2.0 / 3.0 * courant) * curve))


def roll(value, steps):
    steps = steps % value.shape[-1]
    return value if steps == 0 else pltpu.roll(value, steps, 1)


def edge_pair(cells, west, east, lane):
    last = cells.shape[-1]
    minus_two = roll(jnp.where(lane >= last - 2, west, cells), 2)
    minus_one = roll(jnp.where(lane >= last - 1, west, cells), 1)
    plus_one = roll(jnp.where(lane < 1, east, cells), -1)
    plus_two = roll(jnp.where(lane < 2, east, cells), -2)
    left = wide_weight * (minus_one + cells) - narrow_weight * (minus_two + plus_one)
    right = wide_weight * (cells + plus_one) - narrow_weight * (minus_one + plus_two)
    return left, right


def packed_edges(cells, ahead, in_slot):
    minus_one = roll(cells, 1)
    minus_two = roll(cells, 2)
    plus_one = roll(jnp.where(in_slot < 1, ahead, cells), -1)
    plus_two = roll(jnp.where(in_slot < 2, ahead, cells), -2)
    left = wide_weight * (minus_one + cells) - narrow_weight * (minus_two + plus_one)
    right = wide_weight * (cells + plus_one) - narrow_weight * (minus_one + plus_two)
    return left, right


def zonal_kernel(
    sizes, tr, off_in, fr_in, cn_in, after, cn_buf,
    buf, off_buf, fr_buf, west_two, pack, ecol, got_pack, got_ecol, got_far,
    lo_buf, prefix, total, suffix, own_head, halo, east_flux_buf, low_left, low_right, low_sum,
    local_sem, send_sem, recv_sem,
):
    lat_count, lon_count = sizes
    depth, rows, lanes = tr.shape
    groups = rows // SUB
    slots = lanes // RIM
    tiles = pack.shape[0]
    lat, lon = lax.axis_index("lat"), lax.axis_index("lon")
    south_end = lat == 0
    north_end = lat == lat_count - 1
    polar = south_end | north_end
    has_south = lat > 0
    has_north = lat < lat_count - 1

    local = [
        pltpu.make_async_copy(tr, buf.at[0], local_sem.at[0]),
        pltpu.make_async_copy(off_in, off_buf, local_sem.at[1]),
        pltpu.make_async_copy(fr_in, fr_buf, local_sem.at[2]),
        pltpu.make_async_copy(cn_in, cn_buf.at[pl.ds(0, rows)], local_sem.at[3]),
    ]
    for copy in local:
        copy.start()

    def lon_dev(steps):
        return {"lat": lat, "lon": lax.rem(lon + steps + lon_count, lon_count)}

    def lat_dev(steps):
        return {"lat": lax.rem(lat + steps + lat_count, lat_count), "lon": lon}

    barrier = pltpu.get_barrier_semaphore()

    def greet(device):
        pl.semaphore_signal(barrier, inc=1, device_id=device, device_id_type=MESH)

    greet(lon_dev(1))
    greet(lon_dev(-1))
    pl.when(has_south)(lambda: greet(lat_dev(-1)))
    pl.when(has_north)(lambda: greet(lat_dev(1)))

    @pl.when(polar)
    def _():
        for steps in (2, -2, 3, -3):
            greet(lon_dev(steps))

    lane = lax.broadcasted_iota(jnp.int32, (SUB, lanes), 1)
    slot_of = lane // RIM
    in_slot = lane & (RIM - 1)

    for copy in local[:3]:
        copy.wait()

    for tile in range(tiles):
        packed = jnp.zeros((SUB, lanes), jnp.float32)
        for slot in range(slots):
            group, t = divmod(tile * slots + slot, depth)
            if group >= groups:
                break
            cells = buf[0, t, group * SUB : (group + 1) * SUB, :]
            packed = jnp.where(slot_of == slot, roll(cells, RIM * (slot + 1)), packed)
        pack[tile] = packed
    for tile in range(ecol.shape[0]):
        packed = jnp.zeros((SUB, lanes), jnp.float32)
        for slot in range(slots):
            group = tile * slots + slot
            if group >= groups:
                break
            span = slice(group * SUB, (group + 1) * SUB)
            base = slot * RIM
            for t in range(depth):
                at = base + 2 * t
                packed = jnp.where((lane >= at) & (lane < at + 2), roll(buf[0, t, span, :], at), packed)
            at = base + 2 * depth
            packed = jnp.where(lane == at, roll(off_buf[span, :].astype(jnp.float32), at), packed)
            packed = jnp.where(lane == at + 1, roll(fr_buf[span, :], at + 1), packed)
        ecol[tile] = packed

    pl.semaphore_wait(barrier, jnp.where(polar, 7, 4))

    def remote(source, target, index, device):
        return pltpu.make_async_remote_copy(
            src_ref=source, dst_ref=target, send_sem=send_sem.at[index], recv_sem=recv_sem.at[index],
            device_id=device, device_id_type=MESH,
        )

    full_row = jnp.where(south_end, 0, rows - FULL_GROUPS * SUB)
    full_span = pl.ds(pl.multiple_of(full_row, SUB), FULL_GROUPS * SUB)
    polar_row = jnp.where(south_end, 0, rows - POLAR_GROUPS * SUB)
    polar_span = pl.ds(pl.multiple_of(polar_row, SUB), POLAR_GROUPS * SUB)
    far_span = pl.ds(jnp.where(south_end, 0, tiles - 3), 3)
    rim_copies = [
        remote(pack, got_pack, 0, lon_dev(1)),
        remote(ecol, got_ecol, 1, lon_dev(-1)),
    ]
    for copy in rim_copies:
        copy.start()
    polar_copies = [
        remote(tr.at[:, full_span], buf.at[1, :, full_span], 3, lon_dev(1)),
        remote(tr.at[:, polar_span], west_two.at[:, polar_span], 4, lon_dev(2)),
        remote(pack.at[far_span], got_far.at[far_span], 5, lon_dev(3)),
    ]

    @pl.when(polar)
    def _():
        for copy in polar_copies:
            copy.start()

    courant_copy = remote(cn_in.at[pl.ds(0, SUB)], cn_buf.at[pl.ds(rows, SUB)], 2, lat_dev(-1))
    pl.when(has_south)(courant_copy.start)

    row_of = lax.broadcasted_iota(jnp.int32, (lanes, lanes), 0)
    col_of = lax.broadcasted_iota(jnp.int32, (lanes, lanes), 1)
    ones = jnp.ones((lanes, lanes), jnp.float32)
    upto = (row_of <= col_of).astype(jnp.float32)
    prefix_matrix = jnp.concatenate([upto, ones], axis=1).astype(jnp.bfloat16)
    suffix_matrix = (upto - ones).astype(jnp.bfloat16)
    slot_matrix = jnp.where(row_of // RIM == col_of // RIM, upto - ones, 0.0).astype(jnp.bfloat16)

    for t in range(depth):
        both = split_dot(buf[0, t], prefix_matrix)
        prefix[0, t] = both[:, :lanes]
        total[0, t] = both[:, lanes:]
    tail_sum = split_dot(pack[...].reshape(tiles * SUB, lanes), slot_matrix)

    def slot_pattern(tile, turn):
        order = jnp.minimum(tile * slots + ((slot_of + turn) & (slots - 1)), depth * groups - 1)
        group = (order * 13) >> 6
        return (group & (slots - 1)) * RIM, order - depth * group

    def heads(columns, tile):
        base, t = slot_pattern(tile, slots - 1)
        return take(columns[tile * slots // (depth * slots)], base + 2 * t + (lane & 1))

    for tile in range(tiles):
        own_head[tile] = heads(ecol, tile)
    local[3].wait()

    for copy in rim_copies:
        copy.wait()

    got_sum = split_dot(got_pack[...].reshape(tiles * SUB, lanes), slot_matrix)
    for tile in range(tiles):
        base, t = slot_pattern(tile, 0)
        columns = got_ecol[tile * slots // (depth * slots)]
        ahead = heads(got_ecol, tile)
        tail = pack[tile]
        left, right = packed_edges(tail, ahead, in_slot)
        depart = take(columns, base + 2 * depth).astype(jnp.int32)
        courant = take(columns, base + 2 * depth + 1)
        index = (slot_of * RIM + (RIM - 1) - depart) & (lanes - 1)
        span = slice(tile * SUB, (tile + 1) * SUB)
        east_flux_buf[tile] = frac_flux(courant, take(right, index), take(left, index), take(tail, index)) - take(
            tail_sum[span], index
        )
        west = got_pack[tile]
        low_left[tile], low_right[tile] = packed_edges(west, own_head[tile], in_slot)
        low_sum[tile] = got_sum[span]
        halo[tile] = jnp.where(in_slot < 2, ahead, west)

    def finish(t, first, own, flux, east_flux):
        next_flux = roll(jnp.where(lane == 0, east_flux, flux), -1)
        after[t, pl.ds(pl.multiple_of(first + SUB, SUB), SUB), :] = own - (next_flux - flux)

    def near_zonal(group):
        first = pl.multiple_of(group * SUB, SUB)
        span = pl.ds(first, SUB)
        courant = fr_buf[span, :]
        depart = lane - off_buf[span, :] - 1
        in_low = depart < 0
        index = depart & (lanes - 1)
        for t in range(depth):
            order = group * depth + t
            tile, slot = order // slots, lax.rem(order, slots)
            own = buf[0, t, span, :]
            around = take(halo[tile], (lane + RIM * (slot + 1)) & (lanes - 1))
            left, right = edge_pair(own, around, around, lane)
            own_prefix = prefix[0, t, span, :]
            low_index = (depart + RIM * (slot + 1)) & (lanes - 1)

            def pick(table, low_table):
                return jnp.where(in_low, take(low_table[tile], low_index), take(table, index))

            flux = (
                (own_prefix - own)
                - pick(own_prefix, low_sum)
                + frac_flux(courant, pick(right, low_right), pick(left, low_left), pick(own, got_pack))
            )
            east_flux = take(east_flux_buf[tile], jnp.full((SUB, lanes), 0, jnp.int32) + slot * RIM)
            finish(t, first, own, flux, east_flux)

    def is_polar(group):
        return (south_end & (group < POLAR_GROUPS)) | (north_end & (group >= groups - POLAR_GROUPS))

    def full_zonal(group):
        first = pl.multiple_of(group * SUB, SUB)
        span = pl.ds(first, SUB)
        far = jnp.where(is_polar(group), 1, 0)
        off = off_buf[span, :]
        courant = fr_buf[span, :]
        east = got_ecol[group // slots]
        base = lax.rem(group, slots) * RIM
        east_off = take(east, jnp.full((SUB, lanes), 0, jnp.int32) + (base + 2 * depth)).astype(jnp.int32)
        east_courant = take(east, jnp.full((SUB, lanes), 0, jnp.int32) + (base + 2 * depth + 1))
        depart = lane - off - 1 + far * lanes
        in_low = depart < 0
        index = depart & (lanes - 1)
        east_index = (lanes - 1 - east_off + far * lanes) & (lanes - 1)
        for t in range(depth):
            own = buf[0, t, span, :]
            near = buf[far, t, span, :]
            low = lo_buf[t, span, :]
            order = group * depth + t
            beyond = take(got_far[order // slots], (lane + RIM * (lax.rem(order, slots) + 1)) & (lanes - 1))
            ahead = take(east, (lane + (base + 2 * t)) & (lanes - 1))
            ahead = jnp.where(far == 1, own, ahead)
            near_left, near_right = edge_pair(near, low, ahead, lane)
            far_left, far_right = edge_pair(low, beyond, near, lane)
            near_prefix = prefix[far, t, span, :]
            far_total = jnp.where(far == 1, total[far, t, span, :], 0.0)

            def pick(near_table, low_table):
                return jnp.where(in_low, take(low_table, index), take(near_table, index))

            flux = (
                (prefix[0, t, span, :] - own + far_total)
                - pick(near_prefix, suffix[t, span, :])
                + frac_flux(courant, pick(near_right, far_right), pick(near_left, far_left), pick(near, low))
            )
            east_flux = (
                (total[0, t, span, :] + far_total)
                - take(near_prefix, east_index)
                + frac_flux(
                    east_courant, take(near_right, east_index), take(near_left, east_index), take(near, east_index)
                )
            )
            finish(t, first, own, flux, east_flux)

    near_zonal(jnp.where(south_end, groups - 1, 0))
    near_zonal(jnp.where(north_end, 1, jnp.where(south_end, groups - 2, groups - 1)))
    to_south = remote(after.at[:, pl.ds(SUB, SUB)], after.at[:, pl.ds(SUB + rows, SUB)], 6, lat_dev(-1))
    to_north = remote(after.at[:, pl.ds(rows, SUB)], after.at[:, pl.ds(0, SUB)], 7, lat_dev(1))
    pl.when(has_south)(to_south.start)
    pl.when(has_north)(to_north.start)

    inner = jnp.where(south_end, FULL_GROUPS, jnp.where(north_end, 2, 1))
    pairs = jnp.where(polar, (groups - FULL_GROUPS) // 2 - 1, groups // 2 - 1)

    def inner_pair(i, carry):
        near_zonal(inner + 2 * i)
        near_zonal(inner + 2 * i + 1)
        return carry

    lax.fori_loop(0, pairs, inner_pair, 0)

    @pl.when(polar)
    def _():
        for copy in polar_copies:
            copy.wait()
        lo_buf[:, full_span, :] = buf[1, :, full_span, :]
        lo_buf[:, polar_span, :] = west_two[:, polar_span, :]
        for t in range(depth):
            both = split_dot(buf[1, t, polar_span, :], prefix_matrix)
            prefix[1, t, polar_span, :] = both[:, :lanes]
            total[1, t, polar_span, :] = both[:, lanes:]
            suffix[t, full_span, :] = split_dot(lo_buf[t, full_span, :], suffix_matrix)

        def full_pair(i, carry):
            full_zonal(full_row // SUB + 2 * i)
            full_zonal(full_row // SUB + 2 * i + 1)
            return carry

        lax.fori_loop(0, FULL_GROUPS // 2, full_pair, 0)

    @pl.when(has_south)
    def _():
        courant_copy.wait_send()
        to_south.wait_send()
        to_north.wait_recv()

    @pl.when(has_north)
    def _():
        to_north.wait_send()
        to_south.wait_recv()
        courant_copy.wait_recv()

    @pl.when(south_end)
    def _():
        after[:, 0:SUB, :] = jnp.zeros((depth, SUB, lanes), jnp.float32)
        cn_buf[0:1, :] = jnp.zeros((1, lanes), jnp.float32)

    @pl.when(north_end)
    def _():
        after[:, SUB + rows :, :] = jnp.zeros((depth, SUB, lanes), jnp.float32)
        cn_buf[rows:, :] = jnp.zeros((SUB, lanes), jnp.float32)


def merid_kernel(after, cn_buf, out, edge_buf, flux_buf, done, sems):
    depth, rows, lanes = out.shape
    courant = cn_buf[0 : rows + 1, :]
    copies = []
    for t in range(depth):
        edge_buf[t, 0 : rows + 2, :] = wide_weight * (
            after[t, SUB - 2 : SUB + rows, :] + after[t, SUB - 1 : SUB + rows + 1, :]
        ) - narrow_weight * (after[t, SUB - 3 : SUB + rows - 1, :] + after[t, SUB : SUB + rows + 2, :])
        flux_buf[t, 0 : rows + 1, :] = frac_flux(
            courant,
            edge_buf[t, 1 : rows + 2, :],
            edge_buf[t, 0 : rows + 1, :],
            after[t, SUB - 1 : SUB + rows, :],
        )
        done[t] = after[t, SUB : SUB + rows, :] - (flux_buf[t, 1 : rows + 1, :] - flux_buf[t, 0:rows, :])
        copies.append(pltpu.make_async_copy(done.at[t], out.at[t], sems.at[t]))
        copies[-1].start()
    for copy in copies:
        copy.wait()


def on_device(sizes, tracers, offsets, fraction, courant_north):
    tracer_count, level_count, rows, lanes = tracers.shape
    depth = tracer_count * level_count
    f32 = jnp.float32
    groups = rows // SUB
    slots = lanes // RIM
    tiles = -(-(depth * groups) // slots)
    column_tiles = -(-groups // slots)
    anywhere = pl.BlockSpec(memory_space=pl.ANY)
    vmem = pl.BlockSpec(memory_space=pltpu.VMEM)
    packed = pltpu.VMEM((tiles, SUB, lanes), f32)
    columns = pltpu.VMEM((column_tiles, SUB, lanes), f32)
    block = pltpu.VMEM((depth, rows, lanes), f32)
    two_blocks = pltpu.VMEM((2, depth, rows, lanes), f32)
    after, courant = pl.pallas_call(
        functools.partial(zonal_kernel, sizes),
        out_shape=(
            pltpu.VMEM((depth, rows + 2 * SUB, lanes), f32),
            pltpu.VMEM((rows + SUB, lanes), f32),
        ),
        in_specs=[pl.BlockSpec(memory_space=pltpu.HBM)] * 4,
        out_specs=(vmem, vmem),
        scratch_shapes=[
            two_blocks,
            pltpu.VMEM((rows, lanes), jnp.int32),
            pltpu.VMEM((rows, lanes), f32),
            block,
            packed, columns, packed, columns, packed,
            block, two_blocks, two_blocks, block,
            packed, packed, packed, packed, packed, packed,
            pltpu.SemaphoreType.DMA((4,)),
            pltpu.SemaphoreType.DMA((8,)),
            pltpu.SemaphoreType.DMA((8,)),
        ],
        compiler_params=pltpu.CompilerParams(collective_id=0, has_side_effects=True, vmem_limit_bytes=66_633_728),
    )(tracers.reshape(depth, rows, lanes), offsets, fraction, courant_north)
    advected = pl.pallas_call(
        merid_kernel,
        out_shape=jax.ShapeDtypeStruct((depth, rows, lanes), f32),
        in_specs=[vmem, vmem],
        out_specs=anywhere,
        scratch_shapes=[
            pltpu.VMEM((depth, rows + SUB, lanes), f32),
            pltpu.VMEM((depth, rows + SUB, lanes), f32),
            block,
            pltpu.SemaphoreType.DMA((depth,)),
        ],
        compiler_params=pltpu.CompilerParams(vmem_limit_bytes=8 << 20),
    )(after, courant)
    return advected.reshape(tracers.shape)


def solution(mesh):
    placed = (P(None, None, "lat", "lon"), P("lat", "lon"), P("lat", "lon"), P("lat", "lon"))
    return jax.shard_map(
        functools.partial(on_device, (mesh.shape["lat"], mesh.shape["lon"])),
        mesh=mesh,
        in_specs=placed,
        out_specs=P(None, None, "lat", "lon"),
        check_vma=False,
    )
```

```python
import functools

import jax
import jax.numpy as jnp
from jax import lax
from jax.experimental import pallas as pl
from jax.experimental.pallas import tpu as pltpu
from jax.sharding import PartitionSpec as P

wide_weight = 7.0 / 12.0
narrow_weight = 1.0 / 12.0
MESH = pl.DeviceIdType.MESH
SUB = 8
RIM = 16
POLAR_GROUPS = 3
FULL_GROUPS = 6


def take(table, index):
    return jnp.take_along_axis(table, index, axis=1, mode="promise_in_bounds")


def split_dot(value, matrix):
    high = value.astype(jnp.bfloat16)
    low = (value - high.astype(jnp.float32)).astype(jnp.bfloat16)
    return jnp.dot(high, matrix, preferred_element_type=jnp.float32) + jnp.dot(
        low, matrix, preferred_element_type=jnp.float32
    )


def frac_flux(courant, right, left, centre):
    jump = right - left
    curve = 6.0 * (centre - 0.5 * (left + right))
    return courant * (right - 0.5 * courant * (jump - (1.0 - 2.0 / 3.0 * courant) * curve))


def roll(value, steps):
    steps = steps % value.shape[-1]
    return value if steps == 0 else pltpu.roll(value, steps, 1)


def edge_pair(cells, west, east, lane):
    last = cells.shape[-1]
    minus_two = roll(jnp.where(lane >= last - 2, west, cells), 2)
    minus_one = roll(jnp.where(lane >= last - 1, west, cells), 1)
    plus_one = roll(jnp.where(lane < 1, east, cells), -1)
    plus_two = roll(jnp.where(lane < 2, east, cells), -2)
    left = wide_weight * (minus_one + cells) - narrow_weight * (minus_two + plus_one)
    right = wide_weight * (cells + plus_one) - narrow_weight * (minus_one + plus_two)
    return left, right


def packed_edges(cells, ahead, in_slot):
    minus_one = roll(cells, 1)
    minus_two = roll(cells, 2)
    plus_one = roll(jnp.where(in_slot < 1, ahead, cells), -1)
    plus_two = roll(jnp.where(in_slot < 2, ahead, cells), -2)
    left = wide_weight * (minus_one + cells) - narrow_weight * (minus_two + plus_one)
    right = wide_weight * (cells + plus_one) - narrow_weight * (minus_one + plus_two)
    return left, right


def zonal_kernel(
    sizes, tr, off_in, fr_in, cn_in, after, cn_buf,
    buf, off_buf, fr_buf, west_two, pack, ecol, got_pack, got_ecol, got_far,
    lo_buf, prefix, total, suffix, own_head, halo, east_flux_buf, low_left, low_right, low_sum, low_cell,
    local_sem, send_sem, recv_sem,
):
    lat_count, lon_count = sizes
    depth, rows, lanes = tr.shape
    groups = rows // SUB
    slots = lanes // RIM
    tiles = pack.shape[0]
    lat, lon = lax.axis_index("lat"), lax.axis_index("lon")
    south_end = lat == 0
    north_end = lat == lat_count - 1
    polar = south_end | north_end
    has_south = lat > 0
    has_north = lat < lat_count - 1

    local = [
        pltpu.make_async_copy(tr, buf.at[0], local_sem.at[0]),
        pltpu.make_async_copy(off_in, off_buf, local_sem.at[1]),
        pltpu.make_async_copy(fr_in, fr_buf, local_sem.at[2]),
        pltpu.make_async_copy(cn_in, cn_buf.at[pl.ds(0, rows)], local_sem.at[3]),
    ]
    for copy in local:
        copy.start()

    def lon_dev(steps):
        return {"lat": lat, "lon": lax.rem(lon + steps + lon_count, lon_count)}

    def lat_dev(steps):
        return {"lat": lax.rem(lat + steps + lat_count, lat_count), "lon": lon}

    barrier = pltpu.get_barrier_semaphore()

    def greet(device):
        pl.semaphore_signal(barrier, inc=1, device_id=device, device_id_type=MESH)

    greet(lon_dev(1))
    greet(lon_dev(-1))
    pl.when(has_south)(lambda: greet(lat_dev(-1)))
    pl.when(has_north)(lambda: greet(lat_dev(1)))

    @pl.when(polar)
    def _():
        for steps in (2, -2, 3, -3):
            greet(lon_dev(steps))

    lane = lax.broadcasted_iota(jnp.int32, (SUB, lanes), 1)
    slot_of = lane // RIM
    in_slot = lane & (RIM - 1)

    for copy in local[:3]:
        copy.wait()

    for tile in range(tiles):
        packed = jnp.zeros((SUB, lanes), jnp.float32)
        for slot in range(slots):
            group, t = divmod(tile * slots + slot, depth)
            if group >= groups:
                break
            cells = buf[0, t, group * SUB : (group + 1) * SUB, :]
            packed = jnp.where(slot_of == slot, roll(cells, RIM * (slot + 1)), packed)
        pack[tile] = packed
    for tile in range(ecol.shape[0]):
        packed = jnp.zeros((SUB, lanes), jnp.float32)
        for slot in range(slots):
            group = tile * slots + slot
            if group >= groups:
                break
            span = slice(group * SUB, (group + 1) * SUB)
            base = slot * RIM
            for t in range(depth):
                at = base + 2 * t
                packed = jnp.where((lane >= at) & (lane < at + 2), roll(buf[0, t, span, :], at), packed)
            at = base + 2 * depth
            packed = jnp.where(lane == at, roll(off_buf[span, :].astype(jnp.float32), at), packed)
            packed = jnp.where(lane == at + 1, roll(fr_buf[span, :], at + 1), packed)
        ecol[tile] = packed

    pl.semaphore_wait(barrier, jnp.where(polar, 7, 4))

    def remote(source, target, index, device):
        return pltpu.make_async_remote_copy(
            src_ref=source, dst_ref=target, send_sem=send_sem.at[index], recv_sem=recv_sem.at[index],
            device_id=device, device_id_type=MESH,
        )

    full_row = jnp.where(south_end, 0, rows - FULL_GROUPS * SUB)
    full_span = pl.ds(pl.multiple_of(full_row, SUB), FULL_GROUPS * SUB)
    polar_row = jnp.where(south_end, 0, rows - POLAR_GROUPS * SUB)
    polar_span = pl.ds(pl.multiple_of(polar_row, SUB), POLAR_GROUPS * SUB)
    far_span = pl.ds(jnp.where(south_end, 0, tiles - 3), 3)
    rim_copies = [
        remote(pack, got_pack, 0, lon_dev(1)),
        remote(ecol, got_ecol, 1, lon_dev(-1)),
    ]
    for copy in rim_copies:
        copy.start()
    polar_copies = [
        remote(tr.at[:, full_span], buf.at[1, :, full_span], 3, lon_dev(1)),
        remote(tr.at[:, polar_span], west_two.at[:, polar_span], 4, lon_dev(2)),
        remote(pack.at[far_span], got_far.at[far_span], 5, lon_dev(3)),
    ]

    @pl.when(polar)
    def _():
        for copy in polar_copies:
            copy.start()

    courant_copy = remote(cn_in.at[pl.ds(0, SUB)], cn_buf.at[pl.ds(rows, SUB)], 2, lat_dev(-1))
    pl.when(has_south)(courant_copy.start)

    row_of = lax.broadcasted_iota(jnp.int32, (lanes, lanes), 0)
    col_of = lax.broadcasted_iota(jnp.int32, (lanes, lanes), 1)
    ones = jnp.ones((lanes, lanes), jnp.float32)
    upto = (row_of <= col_of).astype(jnp.float32)
    prefix_matrix = jnp.concatenate([upto, ones], axis=1).astype(jnp.bfloat16)
    suffix_matrix = (upto - ones).astype(jnp.bfloat16)
    slot_matrix = jnp.where(row_of // RIM == col_of // RIM, upto - ones, 0.0).astype(jnp.bfloat16)

    for t in range(depth):
        both = split_dot(buf[0, t], prefix_matrix)
        prefix[0, t] = both[:, :lanes]
        total[0, t] = both[:, lanes:]
    tail_sum = split_dot(pack[...].reshape(tiles * SUB, lanes), slot_matrix)

    def slot_pattern(tile, turn):
        order = jnp.minimum(tile * slots + ((slot_of + turn) & (slots - 1)), depth * groups - 1)
        group = (order * 13) >> 6
        return (group & (slots - 1)) * RIM, order - depth * group

    def heads(columns, tile):
        base, t = slot_pattern(tile, slots - 1)
        return take(columns[tile * slots // (depth * slots)], base + 2 * t + (lane & 1))

    for tile in range(tiles):
        own_head[tile] = heads(ecol, tile)
    local[3].wait()

    def arrive():
        for copy in rim_copies:
            copy.wait()
        got_sum = split_dot(got_pack[...].reshape(tiles * SUB, lanes), slot_matrix)
        for tile in range(tiles):
            base, t = slot_pattern(tile, 0)
            columns = got_ecol[tile * slots // (depth * slots)]
            ahead = heads(got_ecol, tile)
            tail = pack[tile]
            left, right = packed_edges(tail, ahead, in_slot)
            depart = take(columns, base + 2 * depth).astype(jnp.int32)
            courant = take(columns, base + 2 * depth + 1)
            index = (slot_of * RIM + (RIM - 1) - depart) & (lanes - 1)
            span = slice(tile * SUB, (tile + 1) * SUB)
            east_flux_buf[tile] = frac_flux(courant, take(right, index), take(left, index), take(tail, index)) - take(
                tail_sum[span], index
            )
            west = got_pack[tile]
            low_left[tile], low_right[tile] = packed_edges(west, own_head[tile], in_slot)
            low_sum[tile] = got_sum[span]
            halo[tile] = jnp.where(in_slot < 2, ahead, west)
            low_cell[tile] = west

    def finish(t, first, own, flux, east_flux):
        next_flux = roll(jnp.where(lane == 0, east_flux, flux), -1)
        after[t, pl.ds(pl.multiple_of(first + SUB, SUB), SUB), :] = own - (next_flux - flux)

    def near_zonal(group):
        first = pl.multiple_of(group * SUB, SUB)
        span = pl.ds(first, SUB)
        courant = fr_buf[span, :]
        depart = lane - off_buf[span, :] - 1
        in_low = depart < 0
        index = depart & (lanes - 1)
        for t in range(depth):
            order = group * depth + t
            tile, slot = order // slots, lax.rem(order, slots)
            own = buf[0, t, span, :]
            around = take(halo[tile], (lane + RIM * (slot + 1)) & (lanes - 1))
            left, right = edge_pair(own, around, around, lane)
            own_prefix = prefix[0, t, span, :]
            low_index = (depart + RIM * (slot + 1)) & (lanes - 1)

            def pick(table, low_table):
                return jnp.where(in_low, take(low_table[tile], low_index), take(table, index))

            flux = (
                (own_prefix - own)
                - pick(own_prefix, low_sum)
                + frac_flux(courant, pick(right, low_right), pick(left, low_left), pick(own, low_cell))
            )
            east_flux = take(east_flux_buf[tile], jnp.full((SUB, lanes), 0, jnp.int32) + slot * RIM)
            finish(t, first, own, flux, east_flux)

    def is_polar(group):
        return (south_end & (group < POLAR_GROUPS)) | (north_end & (group >= groups - POLAR_GROUPS))

    def full_zonal(group):
        first = pl.multiple_of(group * SUB, SUB)
        span = pl.ds(first, SUB)
        far = jnp.where(is_polar(group), 1, 0)
        off = off_buf[span, :]
        courant = fr_buf[span, :]
        east = got_ecol[group // slots]
        base = lax.rem(group, slots) * RIM
        east_off = take(east, jnp.full((SUB, lanes), 0, jnp.int32) + (base + 2 * depth)).astype(jnp.int32)
        east_courant = take(east, jnp.full((SUB, lanes), 0, jnp.int32) + (base + 2 * depth + 1))
        depart = lane - off - 1 + far * lanes
        in_low = depart < 0
        index = depart & (lanes - 1)
        east_index = (lanes - 1 - east_off + far * lanes) & (lanes - 1)
        for t in range(depth):
            own = buf[0, t, span, :]
            near = buf[far, t, span, :]
            low = lo_buf[t, span, :]
            order = group * depth + t
            beyond = take(got_far[order // slots], (lane + RIM * (lax.rem(order, slots) + 1)) & (lanes - 1))
            ahead = take(east, (lane + (base + 2 * t)) & (lanes - 1))
            ahead = jnp.where(far == 1, own, ahead)
            near_left, near_right = edge_pair(near, low, ahead, lane)
            far_left, far_right = edge_pair(low, beyond, near, lane)
            near_prefix = prefix[far, t, span, :]
            far_total = jnp.where(far == 1, total[far, t, span, :], 0.0)

            def pick(near_table, low_table):
                return jnp.where(in_low, take(low_table, index), take(near_table, index))

            flux = (
                (prefix[0, t, span, :] - own + far_total)
                - pick(near_prefix, suffix[t, span, :])
                + frac_flux(courant, pick(near_right, far_right), pick(near_left, far_left), pick(near, low))
            )
            east_flux = (
                (total[0, t, span, :] + far_total)
                - take(near_prefix, east_index)
                + frac_flux(
                    east_courant, take(near_right, east_index), take(near_left, east_index), take(near, east_index)
                )
            )
            finish(t, first, own, flux, east_flux)

    edge_one = jnp.where(south_end, groups - 1, 0)
    edge_two = jnp.where(north_end, 1, jnp.where(south_end, groups - 2, groups - 1))
    to_south = remote(after.at[:, pl.ds(SUB, SUB)], after.at[:, pl.ds(SUB + rows, SUB)], 6, lat_dev(-1))
    to_north = remote(after.at[:, pl.ds(rows, SUB)], after.at[:, pl.ds(0, SUB)], 7, lat_dev(1))
    inner = jnp.where(south_end, FULL_GROUPS, jnp.where(north_end, 2, 1))
    pairs = jnp.where(polar, (groups - FULL_GROUPS) // 2 - 1, groups // 2 - 1)

    def pair(i, carry):
        pl.when(i == 1)(arrive)
        near_zonal(jnp.where(i < 2, edge_one, inner + 2 * i - 4))
        near_zonal(jnp.where(i < 2, edge_two, inner + 2 * i - 3))

        @pl.when(i == 1)
        def _():
            pl.when(has_south)(to_south.start)
            pl.when(has_north)(to_north.start)

        return carry

    lax.fori_loop(0, pairs + 2, pair, 0)

    @pl.when(polar)
    def _():
        for copy in polar_copies:
            copy.wait()
        lo_buf[:, full_span, :] = buf[1, :, full_span, :]
        lo_buf[:, polar_span, :] = west_two[:, polar_span, :]
        for t in range(depth):
            both = split_dot(buf[1, t, polar_span, :], prefix_matrix)
            prefix[1, t, polar_span, :] = both[:, :lanes]
            total[1, t, polar_span, :] = both[:, lanes:]
            suffix[t, full_span, :] = split_dot(lo_buf[t, full_span, :], suffix_matrix)

        def full_pair(i, carry):
            full_zonal(full_row // SUB + 2 * i)
            full_zonal(full_row // SUB + 2 * i + 1)
            return carry

        lax.fori_loop(0, FULL_GROUPS // 2, full_pair, 0)

    @pl.when(has_south)
    def _():
        courant_copy.wait_send()
        to_south.wait_send()
        to_north.wait_recv()

    @pl.when(has_north)
    def _():
        to_north.wait_send()
        to_south.wait_recv()
        courant_copy.wait_recv()

    @pl.when(south_end)
    def _():
        after[:, 0:SUB, :] = jnp.zeros((depth, SUB, lanes), jnp.float32)
        cn_buf[0:1, :] = jnp.zeros((1, lanes), jnp.float32)

    @pl.when(north_end)
    def _():
        after[:, SUB + rows :, :] = jnp.zeros((depth, SUB, lanes), jnp.float32)
        cn_buf[rows:, :] = jnp.zeros((SUB, lanes), jnp.float32)


def merid_kernel(after, cn_buf, out, edge_buf, flux_buf, done, sems):
    depth, rows, lanes = out.shape
    courant = cn_buf[0 : rows + 1, :]
    copies = []
    for t in range(depth):
        edge_buf[t, 0 : rows + 2, :] = wide_weight * (
            after[t, SUB - 2 : SUB + rows, :] + after[t, SUB - 1 : SUB + rows + 1, :]
        ) - narrow_weight * (after[t, SUB - 3 : SUB + rows - 1, :] + after[t, SUB : SUB + rows + 2, :])
        flux_buf[t, 0 : rows + 1, :] = frac_flux(
            courant,
            edge_buf[t, 1 : rows + 2, :],
            edge_buf[t, 0 : rows + 1, :],
            after[t, SUB - 1 : SUB + rows, :],
        )
        done[t] = after[t, SUB : SUB + rows, :] - (flux_buf[t, 1 : rows + 1, :] - flux_buf[t, 0:rows, :])
        copies.append(pltpu.make_async_copy(done.at[t], out.at[t], sems.at[t]))
        copies[-1].start()
    for copy in copies:
        copy.wait()


def on_device(sizes, tracers, offsets, fraction, courant_north):
    tracer_count, level_count, rows, lanes = tracers.shape
    depth = tracer_count * level_count
    f32 = jnp.float32
    groups = rows // SUB
    slots = lanes // RIM
    tiles = -(-(depth * groups) // slots)
    column_tiles = -(-groups // slots)
    anywhere = pl.BlockSpec(memory_space=pl.ANY)
    vmem = pl.BlockSpec(memory_space=pltpu.VMEM)
    packed = pltpu.VMEM((tiles, SUB, lanes), f32)
    columns = pltpu.VMEM((column_tiles, SUB, lanes), f32)
    block = pltpu.VMEM((depth, rows, lanes), f32)
    two_blocks = pltpu.VMEM((2, depth, rows, lanes), f32)
    after, courant = pl.pallas_call(
        functools.partial(zonal_kernel, sizes),
        out_shape=(
            pltpu.VMEM((depth, rows + 2 * SUB, lanes), f32),
            pltpu.VMEM((rows + SUB, lanes), f32),
        ),
        in_specs=[pl.BlockSpec(memory_space=pltpu.HBM)] * 4,
        out_specs=(vmem, vmem),
        scratch_shapes=[
            two_blocks,
            pltpu.VMEM((rows, lanes), jnp.int32),
            pltpu.VMEM((rows, lanes), f32),
            block,
            packed, columns, packed, columns, packed,
            block, two_blocks, two_blocks, block,
            packed, packed, packed, packed, packed, packed, packed,
            pltpu.SemaphoreType.DMA((4,)),
            pltpu.SemaphoreType.DMA((8,)),
            pltpu.SemaphoreType.DMA((8,)),
        ],
        compiler_params=pltpu.CompilerParams(collective_id=0, has_side_effects=True, vmem_limit_bytes=66_633_728),
    )(tracers.reshape(depth, rows, lanes), offsets, fraction, courant_north)
    advected = pl.pallas_call(
        merid_kernel,
        out_shape=jax.ShapeDtypeStruct((depth, rows, lanes), f32),
        in_specs=[vmem, vmem],
        out_specs=anywhere,
        scratch_shapes=[
            pltpu.VMEM((depth, rows + SUB, lanes), f32),
            pltpu.VMEM((depth, rows + SUB, lanes), f32),
            block,
            pltpu.SemaphoreType.DMA((depth,)),
        ],
        compiler_params=pltpu.CompilerParams(vmem_limit_bytes=8 << 20),
    )(after, courant)
    return advected.reshape(tracers.shape)


def solution(mesh):
    placed = (P(None, None, "lat", "lon"), P("lat", "lon"), P("lat", "lon"), P("lat", "lon"))
    return jax.shard_map(
        functools.partial(on_device, (mesh.shape["lat"], mesh.shape["lon"])),
        mesh=mesh,
        in_specs=placed,
        out_specs=P(None, None, "lat", "lon"),
        check_vma=False,
    )
```

```python
import functools

import jax
import jax.numpy as jnp
from jax import lax
from jax.experimental import pallas as pl
from jax.experimental.pallas import tpu as pltpu
from jax.sharding import PartitionSpec as P

wide_weight = 7.0 / 12.0
narrow_weight = 1.0 / 12.0
MESH = pl.DeviceIdType.MESH
SUB = 8
RIM = 16
POLAR_GROUPS = 3
FULL_GROUPS = 6


def take(table, index):
    return jnp.take_along_axis(table, index, axis=1, mode="promise_in_bounds")


def split_dot(value, matrix):
    high = value.astype(jnp.bfloat16)
    low = (value - high.astype(jnp.float32)).astype(jnp.bfloat16)
    return jnp.dot(high, matrix, preferred_element_type=jnp.float32) + jnp.dot(
        low, matrix, preferred_element_type=jnp.float32
    )


def frac_flux(courant, right, left, centre):
    jump = right - left
    curve = 6.0 * (centre - 0.5 * (left + right))
    return courant * (right - 0.5 * courant * (jump - (1.0 - 2.0 / 3.0 * courant) * curve))


def roll(value, steps):
    steps = steps % value.shape[-1]
    return value if steps == 0 else pltpu.roll(value, steps, 1)


def edge_pair(cells, west, east, lane):
    last = cells.shape[-1]
    minus_two = roll(jnp.where(lane >= last - 2, west, cells), 2)
    minus_one = roll(jnp.where(lane >= last - 1, west, cells), 1)
    plus_one = roll(jnp.where(lane < 1, east, cells), -1)
    plus_two = roll(jnp.where(lane < 2, east, cells), -2)
    left = wide_weight * (minus_one + cells) - narrow_weight * (minus_two + plus_one)
    right = wide_weight * (cells + plus_one) - narrow_weight * (minus_one + plus_two)
    return left, right


def packed_edges(cells, ahead, in_slot):
    minus_one = roll(cells, 1)
    minus_two = roll(cells, 2)
    plus_one = roll(jnp.where(in_slot < 1, ahead, cells), -1)
    plus_two = roll(jnp.where(in_slot < 2, ahead, cells), -2)
    left = wide_weight * (minus_one + cells) - narrow_weight * (minus_two + plus_one)
    right = wide_weight * (cells + plus_one) - narrow_weight * (minus_one + plus_two)
    return left, right


def zonal_kernel(
    sizes, tr, off_in, fr_in, cn_in, after, cn_buf,
    buf, off_buf, fr_buf, west_two, pack, ecol, got_pack, got_ecol, got_far,
    lo_buf, prefix, total, suffix, own_head, halo, east_flux_buf, low_left, low_right, low_sum, low_cell,
    local_sem, send_sem, recv_sem,
):
    lat_count, lon_count = sizes
    depth, rows, lanes = tr.shape
    groups = rows // SUB
    slots = lanes // RIM
    tiles = pack.shape[0]
    lat, lon = lax.axis_index("lat"), lax.axis_index("lon")
    south_end = lat == 0
    north_end = lat == lat_count - 1
    polar = south_end | north_end
    has_south = lat > 0
    has_north = lat < lat_count - 1

    local = [
        pltpu.make_async_copy(tr, buf.at[0], local_sem.at[0]),
        pltpu.make_async_copy(off_in, off_buf, local_sem.at[1]),
        pltpu.make_async_copy(fr_in, fr_buf, local_sem.at[2]),
        pltpu.make_async_copy(cn_in, cn_buf.at[pl.ds(0, rows)], local_sem.at[3]),
    ]
    for copy in local:
        copy.start()

    def lon_dev(steps):
        return {"lat": lat, "lon": lax.rem(lon + steps + lon_count, lon_count)}

    def lat_dev(steps):
        return {"lat": lax.rem(lat + steps + lat_count, lat_count), "lon": lon}

    barrier = pltpu.get_barrier_semaphore()

    def greet(device):
        pl.semaphore_signal(barrier, inc=1, device_id=device, device_id_type=MESH)

    greet(lon_dev(1))
    greet(lon_dev(-1))
    pl.when(has_south)(lambda: greet(lat_dev(-1)))
    pl.when(has_north)(lambda: greet(lat_dev(1)))

    @pl.when(polar)
    def _():
        for steps in (2, -2, 3, -3):
            greet(lon_dev(steps))

    lane = lax.broadcasted_iota(jnp.int32, (SUB, lanes), 1)
    slot_of = lane // RIM
    in_slot = lane & (RIM - 1)

    for copy in local[:3]:
        copy.wait()

    for tile in range(tiles):
        packed = jnp.zeros((SUB, lanes), jnp.float32)
        for slot in range(slots):
            group, t = divmod(tile * slots + slot, depth)
            if group >= groups:
                break
            cells = buf[0, t, group * SUB : (group + 1) * SUB, :]
            packed = jnp.where(slot_of == slot, roll(cells, RIM * (slot + 1)), packed)
        pack[tile] = packed
    for tile in range(ecol.shape[0]):
        packed = jnp.zeros((SUB, lanes), jnp.float32)
        for slot in range(slots):
            group = tile * slots + slot
            if group >= groups:
                break
            span = slice(group * SUB, (group + 1) * SUB)
            base = slot * RIM
            for t in range(depth):
                at = base + 2 * t
                packed = jnp.where((lane >= at) & (lane < at + 2), roll(buf[0, t, span, :], at), packed)
            at = base + 2 * depth
            packed = jnp.where(lane == at, roll(off_buf[span, :].astype(jnp.float32), at), packed)
            packed = jnp.where(lane == at + 1, roll(fr_buf[span, :], at + 1), packed)
        ecol[tile] = packed

    pl.semaphore_wait(barrier, jnp.where(polar, 7, 4))

    def remote(source, target, index, device):
        return pltpu.make_async_remote_copy(
            src_ref=source, dst_ref=target, send_sem=send_sem.at[index], recv_sem=recv_sem.at[index],
            device_id=device, device_id_type=MESH,
        )

    full_row = jnp.where(south_end, 0, rows - FULL_GROUPS * SUB)
    full_span = pl.ds(pl.multiple_of(full_row, SUB), FULL_GROUPS * SUB)
    polar_row = jnp.where(south_end, 0, rows - POLAR_GROUPS * SUB)
    polar_span = pl.ds(pl.multiple_of(polar_row, SUB), POLAR_GROUPS * SUB)
    far_span = pl.ds(jnp.where(south_end, 0, tiles - 3), 3)
    edge_parts = ((0, 2), (tiles - 2, tiles))
    inner_part = (2, tiles - 2)

    def rim_copy(part, index):
        span = pl.ds(part[0], part[1] - part[0])
        return remote(pack.at[span], got_pack.at[span], index, lon_dev(1))

    rim_copies = [rim_copy(edge_parts[0], 0), rim_copy(edge_parts[1], 8), remote(ecol, got_ecol, 1, lon_dev(-1))]
    inner_copy = rim_copy(inner_part, 9)
    for copy in rim_copies:
        copy.start()
    inner_copy.start()
    polar_copies = [
        remote(tr.at[:, full_span], buf.at[1, :, full_span], 3, lon_dev(1)),
        remote(tr.at[:, polar_span], west_two.at[:, polar_span], 4, lon_dev(2)),
        remote(pack.at[far_span], got_far.at[far_span], 5, lon_dev(3)),
    ]

    @pl.when(polar)
    def _():
        for copy in polar_copies:
            copy.start()

    courant_copy = remote(cn_in.at[pl.ds(0, SUB)], cn_buf.at[pl.ds(rows, SUB)], 2, lat_dev(-1))
    pl.when(has_south)(courant_copy.start)

    row_of = lax.broadcasted_iota(jnp.int32, (lanes, lanes), 0)
    col_of = lax.broadcasted_iota(jnp.int32, (lanes, lanes), 1)
    ones = jnp.ones((lanes, lanes), jnp.float32)
    upto = (row_of <= col_of).astype(jnp.float32)
    prefix_matrix = jnp.concatenate([upto, ones], axis=1).astype(jnp.bfloat16)
    suffix_matrix = (upto - ones).astype(jnp.bfloat16)
    slot_matrix = jnp.where(row_of // RIM == col_of // RIM, upto - ones, 0.0).astype(jnp.bfloat16)

    for t in range(depth):
        both = split_dot(buf[0, t], prefix_matrix)
        prefix[0, t] = both[:, :lanes]
        total[0, t] = both[:, lanes:]
    tail_sum = split_dot(pack[...].reshape(tiles * SUB, lanes), slot_matrix)

    def slot_pattern(tile, turn):
        order = jnp.minimum(tile * slots + ((slot_of + turn) & (slots - 1)), depth * groups - 1)
        group = (order * 13) >> 6
        return (group & (slots - 1)) * RIM, order - depth * group

    def heads(columns, tile):
        base, t = slot_pattern(tile, slots - 1)
        return take(columns[tile * slots // (depth * slots)], base + 2 * t + (lane & 1))

    for tile in range(tiles):
        own_head[tile] = heads(ecol, tile)
    local[3].wait()

    def rim_tables(part):
        first_tile, last_tile = part
        got_sum = split_dot(got_pack[first_tile:last_tile].reshape((last_tile - first_tile) * SUB, lanes), slot_matrix)
        for tile in range(first_tile, last_tile):
            base, t = slot_pattern(tile, 0)
            columns = got_ecol[tile * slots // (depth * slots)]
            ahead = heads(got_ecol, tile)
            tail = pack[tile]
            left, right = packed_edges(tail, ahead, in_slot)
            depart = take(columns, base + 2 * depth).astype(jnp.int32)
            courant = take(columns, base + 2 * depth + 1)
            index = (slot_of * RIM + (RIM - 1) - depart) & (lanes - 1)
            east_flux_buf[tile] = frac_flux(
                courant, take(right, index), take(left, index), take(tail, index)
            ) - take(tail_sum[tile * SUB : (tile + 1) * SUB], index)
            west = got_pack[tile]
            low_left[tile], low_right[tile] = packed_edges(west, own_head[tile], in_slot)
            low_sum[tile] = got_sum[(tile - first_tile) * SUB : (tile - first_tile + 1) * SUB]
            halo[tile] = jnp.where(in_slot < 2, ahead, west)
            low_cell[tile] = west

    def arrive():
        for copy in rim_copies:
            copy.wait()
        for part in edge_parts:
            rim_tables(part)

    def arrive_rest():
        inner_copy.wait()
        rim_tables(inner_part)

    def finish(t, first, own, flux, east_flux):
        next_flux = roll(jnp.where(lane == 0, east_flux, flux), -1)
        after[t, pl.ds(pl.multiple_of(first + SUB, SUB), SUB), :] = own - (next_flux - flux)

    def near_zonal(group):
        first = pl.multiple_of(group * SUB, SUB)
        span = pl.ds(first, SUB)
        courant = fr_buf[span, :]
        depart = lane - off_buf[span, :] - 1
        in_low = depart < 0
        index = depart & (lanes - 1)
        for t in range(depth):
            order = group * depth + t
            tile, slot = order // slots, lax.rem(order, slots)
            own = buf[0, t, span, :]
            around = take(halo[tile], (lane + RIM * (slot + 1)) & (lanes - 1))
            left, right = edge_pair(own, around, around, lane)
            own_prefix = prefix[0, t, span, :]
            low_index = (depart + RIM * (slot + 1)) & (lanes - 1)

            def pick(table, low_table):
                return jnp.where(in_low, take(low_table[tile], low_index), take(table, index))

            flux = (
                (own_prefix - own)
                - pick(own_prefix, low_sum)
                + frac_flux(courant, pick(right, low_right), pick(left, low_left), pick(own, low_cell))
            )
            east_flux = take(east_flux_buf[tile], jnp.full((SUB, lanes), 0, jnp.int32) + slot * RIM)
            finish(t, first, own, flux, east_flux)

    def is_polar(group):
        return (south_end & (group < POLAR_GROUPS)) | (north_end & (group >= groups - POLAR_GROUPS))

    def full_zonal(group):
        first = pl.multiple_of(group * SUB, SUB)
        span = pl.ds(first, SUB)
        far = jnp.where(is_polar(group), 1, 0)
        off = off_buf[span, :]
        courant = fr_buf[span, :]
        east = got_ecol[group // slots]
        base = lax.rem(group, slots) * RIM
        east_off = take(east, jnp.full((SUB, lanes), 0, jnp.int32) + (base + 2 * depth)).astype(jnp.int32)
        east_courant = take(east, jnp.full((SUB, lanes), 0, jnp.int32) + (base + 2 * depth + 1))
        depart = lane - off - 1 + far * lanes
        in_low = depart < 0
        index = depart & (lanes - 1)
        east_index = (lanes - 1 - east_off + far * lanes) & (lanes - 1)
        for t in range(depth):
            own = buf[0, t, span, :]
            near = buf[far, t, span, :]
            low = lo_buf[t, span, :]
            order = group * depth + t
            beyond = take(got_far[order // slots], (lane + RIM * (lax.rem(order, slots) + 1)) & (lanes - 1))
            ahead = take(east, (lane + (base + 2 * t)) & (lanes - 1))
            ahead = jnp.where(far == 1, own, ahead)
            near_left, near_right = edge_pair(near, low, ahead, lane)
            far_left, far_right = edge_pair(low, beyond, near, lane)
            near_prefix = prefix[far, t, span, :]
            far_total = jnp.where(far == 1, total[far, t, span, :], 0.0)

            def pick(near_table, low_table):
                return jnp.where(in_low, take(low_table, index), take(near_table, index))

            flux = (
                (prefix[0, t, span, :] - own + far_total)
                - pick(near_prefix, suffix[t, span, :])
                + frac_flux(courant, pick(near_right, far_right), pick(near_left, far_left), pick(near, low))
            )
            east_flux = (
                (total[0, t, span, :] + far_total)
                - take(near_prefix, east_index)
                + frac_flux(
                    east_courant, take(near_right, east_index), take(near_left, east_index), take(near, east_index)
                )
            )
            finish(t, first, own, flux, east_flux)

    edge_one = jnp.where(south_end, groups - 1, 0)
    edge_two = jnp.where(north_end, 1, jnp.where(south_end, groups - 2, groups - 1))
    to_south = remote(after.at[:, pl.ds(SUB, SUB)], after.at[:, pl.ds(SUB + rows, SUB)], 6, lat_dev(-1))
    to_north = remote(after.at[:, pl.ds(rows, SUB)], after.at[:, pl.ds(0, SUB)], 7, lat_dev(1))
    inner = jnp.where(south_end, FULL_GROUPS, jnp.where(north_end, 2, 1))
    pairs = jnp.where(polar, (groups - FULL_GROUPS) // 2 - 1, groups // 2 - 1)

    def pair(i, carry):
        pl.when(i == 1)(arrive)
        pl.when(i == 2)(arrive_rest)
        near_zonal(jnp.where(i < 2, edge_one, inner + 2 * i - 4))
        near_zonal(jnp.where(i < 2, edge_two, inner + 2 * i - 3))

        @pl.when(i == 1)
        def _():
            pl.when(has_south)(to_south.start)
            pl.when(has_north)(to_north.start)

        return carry

    lax.fori_loop(0, pairs + 2, pair, 0)

    @pl.when(polar)
    def _():
        for copy in polar_copies:
            copy.wait()
        lo_buf[:, full_span, :] = buf[1, :, full_span, :]
        lo_buf[:, polar_span, :] = west_two[:, polar_span, :]
        for t in range(depth):
            both = split_dot(buf[1, t, polar_span, :], prefix_matrix)
            prefix[1, t, polar_span, :] = both[:, :lanes]
            total[1, t, polar_span, :] = both[:, lanes:]
            suffix[t, full_span, :] = split_dot(lo_buf[t, full_span, :], suffix_matrix)

        def full_pair(i, carry):
            full_zonal(full_row // SUB + 2 * i)
            full_zonal(full_row // SUB + 2 * i + 1)
            return carry

        lax.fori_loop(0, FULL_GROUPS // 2, full_pair, 0)

    @pl.when(has_south)
    def _():
        courant_copy.wait_send()
        to_south.wait_send()
        to_north.wait_recv()

    @pl.when(has_north)
    def _():
        to_north.wait_send()
        to_south.wait_recv()
        courant_copy.wait_recv()

    @pl.when(south_end)
    def _():
        after[:, 0:SUB, :] = jnp.zeros((depth, SUB, lanes), jnp.float32)
        cn_buf[0:1, :] = jnp.zeros((1, lanes), jnp.float32)

    @pl.when(north_end)
    def _():
        after[:, SUB + rows :, :] = jnp.zeros((depth, SUB, lanes), jnp.float32)
        cn_buf[rows:, :] = jnp.zeros((SUB, lanes), jnp.float32)


def merid_kernel(after, cn_buf, out, edge_buf, flux_buf, done, sems):
    depth, rows, lanes = out.shape
    courant = cn_buf[0 : rows + 1, :]
    copies = []
    for t in range(depth):
        edge_buf[t, 0 : rows + 2, :] = wide_weight * (
            after[t, SUB - 2 : SUB + rows, :] + after[t, SUB - 1 : SUB + rows + 1, :]
        ) - narrow_weight * (after[t, SUB - 3 : SUB + rows - 1, :] + after[t, SUB : SUB + rows + 2, :])
        flux_buf[t, 0 : rows + 1, :] = frac_flux(
            courant,
            edge_buf[t, 1 : rows + 2, :],
            edge_buf[t, 0 : rows + 1, :],
            after[t, SUB - 1 : SUB + rows, :],
        )
        done[t] = after[t, SUB : SUB + rows, :] - (flux_buf[t, 1 : rows + 1, :] - flux_buf[t, 0:rows, :])
        copies.append(pltpu.make_async_copy(done.at[t], out.at[t], sems.at[t]))
        copies[-1].start()
    for copy in copies:
        copy.wait()


def on_device(sizes, tracers, offsets, fraction, courant_north):
    tracer_count, level_count, rows, lanes = tracers.shape
    depth = tracer_count * level_count
    f32 = jnp.float32
    groups = rows // SUB
    slots = lanes // RIM
    tiles = -(-(depth * groups) // slots)
    column_tiles = -(-groups // slots)
    anywhere = pl.BlockSpec(memory_space=pl.ANY)
    vmem = pl.BlockSpec(memory_space=pltpu.VMEM)
    packed = pltpu.VMEM((tiles, SUB, lanes), f32)
    columns = pltpu.VMEM((column_tiles, SUB, lanes), f32)
    block = pltpu.VMEM((depth, rows, lanes), f32)
    two_blocks = pltpu.VMEM((2, depth, rows, lanes), f32)
    after, courant = pl.pallas_call(
        functools.partial(zonal_kernel, sizes),
        out_shape=(
            pltpu.VMEM((depth, rows + 2 * SUB, lanes), f32),
            pltpu.VMEM((rows + SUB, lanes), f32),
        ),
        in_specs=[pl.BlockSpec(memory_space=pltpu.HBM)] * 4,
        out_specs=(vmem, vmem),
        scratch_shapes=[
            two_blocks,
            pltpu.VMEM((rows, lanes), jnp.int32),
            pltpu.VMEM((rows, lanes), f32),
            block,
            packed, columns, packed, columns, packed,
            block, two_blocks, two_blocks, block,
            packed, packed, packed, packed, packed, packed, packed,
            pltpu.SemaphoreType.DMA((4,)),
            pltpu.SemaphoreType.DMA((10,)),
            pltpu.SemaphoreType.DMA((10,)),
        ],
        compiler_params=pltpu.CompilerParams(collective_id=0, has_side_effects=True, vmem_limit_bytes=66_633_728),
    )(tracers.reshape(depth, rows, lanes), offsets, fraction, courant_north)
    advected = pl.pallas_call(
        merid_kernel,
        out_shape=jax.ShapeDtypeStruct((depth, rows, lanes), f32),
        in_specs=[vmem, vmem],
        out_specs=anywhere,
        scratch_shapes=[
            pltpu.VMEM((depth, rows + SUB, lanes), f32),
            pltpu.VMEM((depth, rows + SUB, lanes), f32),
            block,
            pltpu.SemaphoreType.DMA((depth,)),
        ],
        compiler_params=pltpu.CompilerParams(vmem_limit_bytes=8 << 20),
    )(after, courant)
    return advected.reshape(tracers.shape)


def solution(mesh):
    placed = (P(None, None, "lat", "lon"), P("lat", "lon"), P("lat", "lon"), P("lat", "lon"))
    return jax.shard_map(
        functools.partial(on_device, (mesh.shape["lat"], mesh.shape["lon"])),
        mesh=mesh,
        in_specs=placed,
        out_specs=P(None, None, "lat", "lon"),
        check_vma=False,
    )
```

```python
import functools

import jax
import jax.numpy as jnp
from jax import lax
from jax.experimental import pallas as pl
from jax.experimental.pallas import tpu as pltpu
from jax.sharding import PartitionSpec as P

wide_weight = 7.0 / 12.0
narrow_weight = 1.0 / 12.0
MESH = pl.DeviceIdType.MESH
SUB = 8
RIM = 16
POLAR_GROUPS = 3
FULL_GROUPS = 6


def take(table, index):
    return jnp.take_along_axis(table, index, axis=1, mode="promise_in_bounds")


def split_dot(value, matrix):
    high = value.astype(jnp.bfloat16)
    low = (value - high.astype(jnp.float32)).astype(jnp.bfloat16)
    return jnp.dot(high, matrix, preferred_element_type=jnp.float32) + jnp.dot(
        low, matrix, preferred_element_type=jnp.float32
    )


def frac_flux(courant, right, left, centre):
    jump = right - left
    curve = 6.0 * (centre - 0.5 * (left + right))
    return courant * (right - 0.5 * courant * (jump - (1.0 - 2.0 / 3.0 * courant) * curve))


def roll(value, steps):
    steps = steps % value.shape[-1]
    return value if steps == 0 else pltpu.roll(value, steps, 1)


def edge_pair(cells, west, east, lane):
    last = cells.shape[-1]
    minus_two = roll(jnp.where(lane >= last - 2, west, cells), 2)
    minus_one = roll(jnp.where(lane >= last - 1, west, cells), 1)
    plus_one = roll(jnp.where(lane < 1, east, cells), -1)
    plus_two = roll(jnp.where(lane < 2, east, cells), -2)
    left = wide_weight * (minus_one + cells) - narrow_weight * (minus_two + plus_one)
    right = wide_weight * (cells + plus_one) - narrow_weight * (minus_one + plus_two)
    return left, right


def packed_edges(cells, ahead, in_slot):
    minus_one = roll(cells, 1)
    minus_two = roll(cells, 2)
    plus_one = roll(jnp.where(in_slot < 1, ahead, cells), -1)
    plus_two = roll(jnp.where(in_slot < 2, ahead, cells), -2)
    left = wide_weight * (minus_one + cells) - narrow_weight * (minus_two + plus_one)
    right = wide_weight * (cells + plus_one) - narrow_weight * (minus_one + plus_two)
    return left, right


def step_kernel(
    sizes, tr, off_in, fr_in, cn_in, done,
    after, cn_buf, edge_buf, flux_buf, buf, off_buf, fr_buf, west_two, pack, ecol, got_pack, got_ecol, got_far,
    lo_buf, prefix, total, suffix, own_head, halo, east_flux_buf, low_left, low_right, low_sum, low_cell,
    local_sem, send_sem, recv_sem,
):
    lat_count, lon_count = sizes
    depth, rows, lanes = tr.shape
    groups = rows // SUB
    slots = lanes // RIM
    tiles = pack.shape[0]
    lat, lon = lax.axis_index("lat"), lax.axis_index("lon")
    south_end = lat == 0
    north_end = lat == lat_count - 1
    polar = south_end | north_end
    has_south = lat > 0
    has_north = lat < lat_count - 1

    local = [
        pltpu.make_async_copy(tr, buf.at[0], local_sem.at[0]),
        pltpu.make_async_copy(off_in, off_buf, local_sem.at[1]),
        pltpu.make_async_copy(fr_in, fr_buf, local_sem.at[2]),
        pltpu.make_async_copy(cn_in, cn_buf.at[pl.ds(0, rows)], local_sem.at[3]),
    ]
    for copy in local:
        copy.start()

    def lon_dev(steps):
        return {"lat": lat, "lon": lax.rem(lon + steps + lon_count, lon_count)}

    def lat_dev(steps):
        return {"lat": lax.rem(lat + steps + lat_count, lat_count), "lon": lon}

    barrier = pltpu.get_barrier_semaphore()

    def greet(device):
        pl.semaphore_signal(barrier, inc=1, device_id=device, device_id_type=MESH)

    greet(lon_dev(1))
    greet(lon_dev(-1))
    pl.when(has_south)(lambda: greet(lat_dev(-1)))
    pl.when(has_north)(lambda: greet(lat_dev(1)))

    @pl.when(polar)
    def _():
        for steps in (2, -2, 3, -3):
            greet(lon_dev(steps))

    lane = lax.broadcasted_iota(jnp.int32, (SUB, lanes), 1)
    slot_of = lane // RIM
    in_slot = lane & (RIM - 1)

    for copy in local[:3]:
        copy.wait()

    for tile in range(tiles):
        packed = jnp.zeros((SUB, lanes), jnp.float32)
        for slot in range(slots):
            group, t = divmod(tile * slots + slot, depth)
            if group >= groups:
                break
            cells = buf[0, t, group * SUB : (group + 1) * SUB, :]
            packed = jnp.where(slot_of == slot, roll(cells, RIM * (slot + 1)), packed)
        pack[tile] = packed
    for tile in range(ecol.shape[0]):
        packed = jnp.zeros((SUB, lanes), jnp.float32)
        for slot in range(slots):
            group = tile * slots + slot
            if group >= groups:
                break
            span = slice(group * SUB, (group + 1) * SUB)
            base = slot * RIM
            for t in range(depth):
                at = base + 2 * t
                packed = jnp.where((lane >= at) & (lane < at + 2), roll(buf[0, t, span, :], at), packed)
            at = base + 2 * depth
            packed = jnp.where(lane == at, roll(off_buf[span, :].astype(jnp.float32), at), packed)
            packed = jnp.where(lane == at + 1, roll(fr_buf[span, :], at + 1), packed)
        ecol[tile] = packed

    pl.semaphore_wait(barrier, jnp.where(polar, 7, 4))

    def remote(source, target, index, device):
        return pltpu.make_async_remote_copy(
            src_ref=source, dst_ref=target, send_sem=send_sem.at[index], recv_sem=recv_sem.at[index],
            device_id=device, device_id_type=MESH,
        )

    full_row = jnp.where(south_end, 0, rows - FULL_GROUPS * SUB)
    full_span = pl.ds(pl.multiple_of(full_row, SUB), FULL_GROUPS * SUB)
    polar_row = jnp.where(south_end, 0, rows - POLAR_GROUPS * SUB)
    polar_span = pl.ds(pl.multiple_of(polar_row, SUB), POLAR_GROUPS * SUB)
    far_span = pl.ds(jnp.where(south_end, 0, tiles - 3), 3)
    edge_parts = ((0, 2), (tiles - 2, tiles))
    inner_part = (2, tiles - 2)

    def rim_copy(part, index):
        span = pl.ds(part[0], part[1] - part[0])
        return remote(pack.at[span], got_pack.at[span], index, lon_dev(1))

    rim_copies = [rim_copy(edge_parts[0], 0), rim_copy(edge_parts[1], 8), remote(ecol, got_ecol, 1, lon_dev(-1))]
    inner_copy = rim_copy(inner_part, 9)
    for copy in rim_copies:
        copy.start()
    inner_copy.start()
    polar_copies = [
        remote(tr.at[:, full_span], buf.at[1, :, full_span], 3, lon_dev(1)),
        remote(tr.at[:, polar_span], west_two.at[:, polar_span], 4, lon_dev(2)),
        remote(pack.at[far_span], got_far.at[far_span], 5, lon_dev(3)),
    ]

    @pl.when(polar)
    def _():
        for copy in polar_copies:
            copy.start()

    courant_copy = remote(cn_in.at[pl.ds(0, SUB)], cn_buf.at[pl.ds(rows, SUB)], 2, lat_dev(-1))
    pl.when(has_south)(courant_copy.start)

    row_of = lax.broadcasted_iota(jnp.int32, (lanes, lanes), 0)
    col_of = lax.broadcasted_iota(jnp.int32, (lanes, lanes), 1)
    ones = jnp.ones((lanes, lanes), jnp.float32)
    upto = (row_of <= col_of).astype(jnp.float32)
    prefix_matrix = jnp.concatenate([upto, ones], axis=1).astype(jnp.bfloat16)
    suffix_matrix = (upto - ones).astype(jnp.bfloat16)
    slot_matrix = jnp.where(row_of // RIM == col_of // RIM, upto - ones, 0.0).astype(jnp.bfloat16)

    for t in range(depth):
        both = split_dot(buf[0, t], prefix_matrix)
        prefix[0, t] = both[:, :lanes]
        total[0, t] = both[:, lanes:]
    tail_sum = split_dot(pack[...].reshape(tiles * SUB, lanes), slot_matrix)

    def slot_pattern(tile, turn):
        order = jnp.minimum(tile * slots + ((slot_of + turn) & (slots - 1)), depth * groups - 1)
        group = (order * 13) >> 6
        return (group & (slots - 1)) * RIM, order - depth * group

    def heads(columns, tile):
        base, t = slot_pattern(tile, slots - 1)
        return take(columns[tile * slots // (depth * slots)], base + 2 * t + (lane & 1))

    for tile in range(tiles):
        own_head[tile] = heads(ecol, tile)
    local[3].wait()

    def rim_tables(part):
        first_tile, last_tile = part
        got_sum = split_dot(got_pack[first_tile:last_tile].reshape((last_tile - first_tile) * SUB, lanes), slot_matrix)
        for tile in range(first_tile, last_tile):
            base, t = slot_pattern(tile, 0)
            columns = got_ecol[tile * slots // (depth * slots)]
            ahead = heads(got_ecol, tile)
            tail = pack[tile]
            left, right = packed_edges(tail, ahead, in_slot)
            depart = take(columns, base + 2 * depth).astype(jnp.int32)
            courant = take(columns, base + 2 * depth + 1)
            index = (slot_of * RIM + (RIM - 1) - depart) & (lanes - 1)
            east_flux_buf[tile] = frac_flux(
                courant, take(right, index), take(left, index), take(tail, index)
            ) - take(tail_sum[tile * SUB : (tile + 1) * SUB], index)
            west = got_pack[tile]
            low_left[tile], low_right[tile] = packed_edges(west, own_head[tile], in_slot)
            low_sum[tile] = got_sum[(tile - first_tile) * SUB : (tile - first_tile + 1) * SUB]
            halo[tile] = jnp.where(in_slot < 2, ahead, west)
            low_cell[tile] = west

    def arrive():
        for copy in rim_copies:
            copy.wait()
        for part in edge_parts:
            rim_tables(part)

    def arrive_rest():
        inner_copy.wait()
        rim_tables(inner_part)

    def finish(t, first, own, flux, east_flux):
        next_flux = roll(jnp.where(lane == 0, east_flux, flux), -1)
        after[t, pl.ds(pl.multiple_of(first + SUB, SUB), SUB), :] = own - (next_flux - flux)

    def near_zonal(group):
        first = pl.multiple_of(group * SUB, SUB)
        span = pl.ds(first, SUB)
        courant = fr_buf[span, :]
        depart = lane - off_buf[span, :] - 1
        in_low = depart < 0
        index = depart & (lanes - 1)
        for t in range(depth):
            order = group * depth + t
            tile, slot = order // slots, lax.rem(order, slots)
            own = buf[0, t, span, :]
            around = take(halo[tile], (lane + RIM * (slot + 1)) & (lanes - 1))
            left, right = edge_pair(own, around, around, lane)
            own_prefix = prefix[0, t, span, :]
            low_index = (depart + RIM * (slot + 1)) & (lanes - 1)

            def pick(table, low_table):
                return jnp.where(in_low, take(low_table[tile], low_index), take(table, index))

            flux = (
                (own_prefix - own)
                - pick(own_prefix, low_sum)
                + frac_flux(courant, pick(right, low_right), pick(left, low_left), pick(own, low_cell))
            )
            east_flux = take(east_flux_buf[tile], jnp.full((SUB, lanes), 0, jnp.int32) + slot * RIM)
            finish(t, first, own, flux, east_flux)

    def is_polar(group):
        return (south_end & (group < POLAR_GROUPS)) | (north_end & (group >= groups - POLAR_GROUPS))

    def full_zonal(group):
        first = pl.multiple_of(group * SUB, SUB)
        span = pl.ds(first, SUB)
        far = jnp.where(is_polar(group), 1, 0)
        off = off_buf[span, :]
        courant = fr_buf[span, :]
        east = got_ecol[group // slots]
        base = lax.rem(group, slots) * RIM
        east_off = take(east, jnp.full((SUB, lanes), 0, jnp.int32) + (base + 2 * depth)).astype(jnp.int32)
        east_courant = take(east, jnp.full((SUB, lanes), 0, jnp.int32) + (base + 2 * depth + 1))
        depart = lane - off - 1 + far * lanes
        in_low = depart < 0
        index = depart & (lanes - 1)
        east_index = (lanes - 1 - east_off + far * lanes) & (lanes - 1)
        for t in range(depth):
            own = buf[0, t, span, :]
            near = buf[far, t, span, :]
            low = lo_buf[t, span, :]
            order = group * depth + t
            beyond = take(got_far[order // slots], (lane + RIM * (lax.rem(order, slots) + 1)) & (lanes - 1))
            ahead = take(east, (lane + (base + 2 * t)) & (lanes - 1))
            ahead = jnp.where(far == 1, own, ahead)
            near_left, near_right = edge_pair(near, low, ahead, lane)
            far_left, far_right = edge_pair(low, beyond, near, lane)
            near_prefix = prefix[far, t, span, :]
            far_total = jnp.where(far == 1, total[far, t, span, :], 0.0)

            def pick(near_table, low_table):
                return jnp.where(in_low, take(low_table, index), take(near_table, index))

            flux = (
                (prefix[0, t, span, :] - own + far_total)
                - pick(near_prefix, suffix[t, span, :])
                + frac_flux(courant, pick(near_right, far_right), pick(near_left, far_left), pick(near, low))
            )
            east_flux = (
                (total[0, t, span, :] + far_total)
                - take(near_prefix, east_index)
                + frac_flux(
                    east_courant, take(near_right, east_index), take(near_left, east_index), take(near, east_index)
                )
            )
            finish(t, first, own, flux, east_flux)

    edge_one = jnp.where(south_end, groups - 1, 0)
    edge_two = jnp.where(north_end, 1, jnp.where(south_end, groups - 2, groups - 1))
    to_south = remote(after.at[:, pl.ds(SUB, SUB)], after.at[:, pl.ds(SUB + rows, SUB)], 6, lat_dev(-1))
    to_north = remote(after.at[:, pl.ds(rows, SUB)], after.at[:, pl.ds(0, SUB)], 7, lat_dev(1))
    inner = jnp.where(south_end, FULL_GROUPS, jnp.where(north_end, 2, 1))
    pairs = jnp.where(polar, (groups - FULL_GROUPS) // 2 - 1, groups // 2 - 1)

    def pair(i, carry):
        pl.when(i == 1)(arrive)
        pl.when(i == 2)(arrive_rest)
        near_zonal(jnp.where(i < 2, edge_one, inner + 2 * i - 4))
        near_zonal(jnp.where(i < 2, edge_two, inner + 2 * i - 3))

        @pl.when(i == 1)
        def _():
            pl.when(has_south)(to_south.start)
            pl.when(has_north)(to_north.start)

        return carry

    lax.fori_loop(0, pairs + 2, pair, 0)

    @pl.when(polar)
    def _():
        for copy in polar_copies:
            copy.wait()
        lo_buf[:, full_span, :] = buf[1, :, full_span, :]
        lo_buf[:, polar_span, :] = west_two[:, polar_span, :]
        for t in range(depth):
            both = split_dot(buf[1, t, polar_span, :], prefix_matrix)
            prefix[1, t, polar_span, :] = both[:, :lanes]
            total[1, t, polar_span, :] = both[:, lanes:]
            suffix[t, full_span, :] = split_dot(lo_buf[t, full_span, :], suffix_matrix)

        def full_pair(i, carry):
            full_zonal(full_row // SUB + 2 * i)
            full_zonal(full_row // SUB + 2 * i + 1)
            return carry

        lax.fori_loop(0, FULL_GROUPS // 2, full_pair, 0)

    def merid(t, first, count):
        at = first + SUB
        edge_buf[t, at - 1 : at + count + 1, :] = wide_weight * (
            after[t, at - 2 : at + count, :] + after[t, at - 1 : at + count + 1, :]
        ) - narrow_weight * (after[t, at - 3 : at + count - 1, :] + after[t, at : at + count + 2, :])
        flux_buf[t, first : first + count + 1, :] = frac_flux(
            cn_buf[first : first + count + 1, :],
            edge_buf[t, at : at + count + 1, :],
            edge_buf[t, at - 1 : at + count, :],
            after[t, at - 1 : at + count, :],
        )
        done[t, first : first + count, :] = after[t, at : at + count, :] - (
            flux_buf[t, first + 1 : first + count + 1, :] - flux_buf[t, first : first + count, :]
        )

    def merid_inner(t, carry):
        merid(t, SUB, rows - 2 * SUB)
        return carry

    lax.fori_loop(0, depth, merid_inner, 0)

    @pl.when(has_south)
    def _():
        courant_copy.wait_send()
        to_south.wait_send()
        to_north.wait_recv()

    @pl.when(has_north)
    def _():
        to_north.wait_send()
        to_south.wait_recv()
        courant_copy.wait_recv()

    @pl.when(south_end)
    def _():
        after[:, 0:SUB, :] = jnp.zeros((depth, SUB, lanes), jnp.float32)
        cn_buf[0:1, :] = jnp.zeros((1, lanes), jnp.float32)

    @pl.when(north_end)
    def _():
        after[:, SUB + rows :, :] = jnp.zeros((depth, SUB, lanes), jnp.float32)
        cn_buf[rows:, :] = jnp.zeros((SUB, lanes), jnp.float32)

    def merid_rim(t, carry):
        merid(t, 0, SUB)
        merid(t, rows - SUB, SUB)
        return carry

    lax.fori_loop(0, depth, merid_rim, 0)


def store_kernel(done, out, sem):
    copy = pltpu.make_async_copy(done, out, sem)
    copy.start()
    copy.wait()


def on_device(sizes, tracers, offsets, fraction, courant_north):
    tracer_count, level_count, rows, lanes = tracers.shape
    depth = tracer_count * level_count
    f32 = jnp.float32
    groups = rows // SUB
    slots = lanes // RIM
    tiles = -(-(depth * groups) // slots)
    column_tiles = -(-groups // slots)
    anywhere = pl.BlockSpec(memory_space=pl.ANY)
    vmem = pl.BlockSpec(memory_space=pltpu.VMEM)
    packed = pltpu.VMEM((tiles, SUB, lanes), f32)
    columns = pltpu.VMEM((column_tiles, SUB, lanes), f32)
    block = pltpu.VMEM((depth, rows, lanes), f32)
    two_blocks = pltpu.VMEM((2, depth, rows, lanes), f32)
    done = pl.pallas_call(
        functools.partial(step_kernel, sizes),
        out_shape=pltpu.VMEM((depth, rows, lanes), f32),
        in_specs=[pl.BlockSpec(memory_space=pltpu.HBM)] * 4,
        out_specs=vmem,
        scratch_shapes=[
            pltpu.VMEM((depth, rows + 2 * SUB, lanes), f32),
            pltpu.VMEM((rows + SUB, lanes), f32),
            pltpu.VMEM((depth, rows + 2 * SUB, lanes), f32),
            pltpu.VMEM((depth, rows + SUB, lanes), f32),
            two_blocks,
            pltpu.VMEM((rows, lanes), jnp.int32),
            pltpu.VMEM((rows, lanes), f32),
            block,
            packed, columns, packed, columns, packed,
            block, two_blocks, two_blocks, block,
            packed, packed, packed, packed, packed, packed, packed,
            pltpu.SemaphoreType.DMA((4,)),
            pltpu.SemaphoreType.DMA((10,)),
            pltpu.SemaphoreType.DMA((10,)),
        ],
        compiler_params=pltpu.CompilerParams(collective_id=0, has_side_effects=True, vmem_limit_bytes=66_747_392),
    )(tracers.reshape(depth, rows, lanes), offsets, fraction, courant_north)
    advected = pl.pallas_call(
        store_kernel,
        out_shape=jax.ShapeDtypeStruct((depth, rows, lanes), f32),
        in_specs=[vmem],
        out_specs=anywhere,
        scratch_shapes=[pltpu.SemaphoreType.DMA],
        compiler_params=pltpu.CompilerParams(vmem_limit_bytes=8 << 20),
    )(done)
    return advected.reshape(tracers.shape)


def solution(mesh):
    placed = (P(None, None, "lat", "lon"), P("lat", "lon"), P("lat", "lon"), P("lat", "lon"))
    return jax.shard_map(
        functools.partial(on_device, (mesh.shape["lat"], mesh.shape["lon"])),
        mesh=mesh,
        in_specs=placed,
        out_specs=P(None, None, "lat", "lon"),
        check_vma=False,
    )
```

```python
import functools

import jax
import jax.numpy as jnp
from jax import lax
from jax.experimental import pallas as pl
from jax.experimental.pallas import tpu as pltpu
from jax.sharding import PartitionSpec as P

wide_weight = 7.0 / 12.0
narrow_weight = 1.0 / 12.0
MESH = pl.DeviceIdType.MESH
SUB = 8
RIM = 16
POLAR_GROUPS = 3
FULL_GROUPS = 6


def take(table, index):
    return jnp.take_along_axis(table, index, axis=1, mode="promise_in_bounds")


def split_dot(value, matrix):
    high = value.astype(jnp.bfloat16)
    low = (value - high.astype(jnp.float32)).astype(jnp.bfloat16)
    return jnp.dot(high, matrix, preferred_element_type=jnp.float32) + jnp.dot(
        low, matrix, preferred_element_type=jnp.float32
    )


def frac_flux(courant, right, left, centre):
    jump = right - left
    curve = 6.0 * (centre - 0.5 * (left + right))
    return courant * (right - 0.5 * courant * (jump - (1.0 - 2.0 / 3.0 * courant) * curve))


def roll(value, steps):
    steps = steps % value.shape[-1]
    return value if steps == 0 else pltpu.roll(value, steps, 1)


def edge_pair(cells, west, east, lane):
    last = cells.shape[-1]
    minus_two = roll(jnp.where(lane >= last - 2, west, cells), 2)
    minus_one = roll(jnp.where(lane >= last - 1, west, cells), 1)
    plus_one = roll(jnp.where(lane < 1, east, cells), -1)
    plus_two = roll(jnp.where(lane < 2, east, cells), -2)
    left = wide_weight * (minus_one + cells) - narrow_weight * (minus_two + plus_one)
    right = wide_weight * (cells + plus_one) - narrow_weight * (minus_one + plus_two)
    return left, right


def packed_edges(cells, ahead, in_slot):
    minus_one = roll(cells, 1)
    minus_two = roll(cells, 2)
    plus_one = roll(jnp.where(in_slot < 1, ahead, cells), -1)
    plus_two = roll(jnp.where(in_slot < 2, ahead, cells), -2)
    left = wide_weight * (minus_one + cells) - narrow_weight * (minus_two + plus_one)
    right = wide_weight * (cells + plus_one) - narrow_weight * (minus_one + plus_two)
    return left, right


def step_kernel(
    sizes, tr, off_in, fr_in, cn_in, done,
    after, cn_buf, edge_buf, flux_buf, buf, off_buf, fr_buf, west_two, pack, ecol, got_pack, got_ecol, got_far,
    lo_buf, prefix, total, suffix, own_head, halo, east_flux_buf, low_left, low_right, low_sum, low_cell,
    local_sem, send_sem, recv_sem,
):
    lat_count, lon_count = sizes
    depth, rows, lanes = tr.shape
    groups = rows // SUB
    slots = lanes // RIM
    tiles = pack.shape[0]
    lat, lon = lax.axis_index("lat"), lax.axis_index("lon")
    south_end = lat == 0
    north_end = lat == lat_count - 1
    polar = south_end | north_end
    has_south = lat > 0
    has_north = lat < lat_count - 1

    local = [
        pltpu.make_async_copy(tr, buf.at[0], local_sem.at[0]),
        pltpu.make_async_copy(off_in, off_buf, local_sem.at[1]),
        pltpu.make_async_copy(fr_in, fr_buf, local_sem.at[2]),
        pltpu.make_async_copy(cn_in, cn_buf.at[pl.ds(0, rows)], local_sem.at[3]),
    ]
    for copy in local:
        copy.start()

    def lon_dev(steps):
        return {"lat": lat, "lon": lax.rem(lon + steps + lon_count, lon_count)}

    def lat_dev(steps):
        return {"lat": lax.rem(lat + steps + lat_count, lat_count), "lon": lon}

    barrier = pltpu.get_barrier_semaphore()

    def greet(device):
        pl.semaphore_signal(barrier, inc=1, device_id=device, device_id_type=MESH)

    greet(lon_dev(1))
    greet(lon_dev(-1))
    pl.when(has_south)(lambda: greet(lat_dev(-1)))
    pl.when(has_north)(lambda: greet(lat_dev(1)))

    @pl.when(polar)
    def _():
        for steps in (2, -2, 3, -3):
            greet(lon_dev(steps))

    lane = lax.broadcasted_iota(jnp.int32, (SUB, lanes), 1)
    slot_of = lane // RIM
    in_slot = lane & (RIM - 1)

    for copy in local[:3]:
        copy.wait()

    for tile in range(tiles):
        packed = jnp.zeros((SUB, lanes), jnp.float32)
        for slot in range(slots):
            group, t = divmod(tile * slots + slot, depth)
            if group >= groups:
                break
            cells = buf[0, t, group * SUB : (group + 1) * SUB, :]
            packed = jnp.where(slot_of == slot, roll(cells, RIM * (slot + 1)), packed)
        pack[tile] = packed
    for tile in range(ecol.shape[0]):
        packed = jnp.zeros((SUB, lanes), jnp.float32)
        for slot in range(slots):
            group = tile * slots + slot
            if group >= groups:
                break
            span = slice(group * SUB, (group + 1) * SUB)
            base = slot * RIM
            for t in range(depth):
                at = base + 2 * t
                packed = jnp.where((lane >= at) & (lane < at + 2), roll(buf[0, t, span, :], at), packed)
            at = base + 2 * depth
            packed = jnp.where(lane == at, roll(off_buf[span, :].astype(jnp.float32), at), packed)
            packed = jnp.where(lane == at + 1, roll(fr_buf[span, :], at + 1), packed)
        ecol[tile] = packed

    pl.semaphore_wait(barrier, jnp.where(polar, 7, 4))

    def remote(source, target, index, device):
        return pltpu.make_async_remote_copy(
            src_ref=source, dst_ref=target, send_sem=send_sem.at[index], recv_sem=recv_sem.at[index],
            device_id=device, device_id_type=MESH,
        )

    full_row = jnp.where(south_end, 0, rows - FULL_GROUPS * SUB)
    full_span = pl.ds(pl.multiple_of(full_row, SUB), FULL_GROUPS * SUB)
    polar_row = jnp.where(south_end, 0, rows - POLAR_GROUPS * SUB)
    polar_span = pl.ds(pl.multiple_of(polar_row, SUB), POLAR_GROUPS * SUB)
    far_span = pl.ds(jnp.where(south_end, 0, tiles - 3), 3)
    edge_parts = ((0, 2), (tiles - 2, tiles))
    inner_part = (2, tiles - 2)

    def rim_copy(part, index):
        span = pl.ds(part[0], part[1] - part[0])
        return remote(pack.at[span], got_pack.at[span], index, lon_dev(1))

    rim_copies = [rim_copy(edge_parts[0], 0), rim_copy(edge_parts[1], 8), remote(ecol, got_ecol, 1, lon_dev(-1))]
    inner_copy = rim_copy(inner_part, 9)
    for copy in rim_copies:
        copy.start()
    inner_copy.start()
    polar_copies = [
        remote(tr.at[:, full_span], buf.at[1, :, full_span], 3, lon_dev(1)),
        remote(tr.at[:, polar_span], west_two.at[:, polar_span], 4, lon_dev(2)),
        remote(pack.at[far_span], got_far.at[far_span], 5, lon_dev(3)),
    ]

    @pl.when(polar)
    def _():
        for copy in polar_copies:
            copy.start()

    courant_copy = remote(cn_in.at[pl.ds(0, SUB)], cn_buf.at[pl.ds(rows, SUB)], 2, lat_dev(-1))
    pl.when(has_south)(courant_copy.start)

    row_of = lax.broadcasted_iota(jnp.int32, (lanes, lanes), 0)
    col_of = lax.broadcasted_iota(jnp.int32, (lanes, lanes), 1)
    ones = jnp.ones((lanes, lanes), jnp.float32)
    upto = (row_of <= col_of).astype(jnp.float32)
    prefix_matrix = jnp.concatenate([upto, ones], axis=1).astype(jnp.bfloat16)
    suffix_matrix = (upto - ones).astype(jnp.bfloat16)
    slot_matrix = jnp.where(row_of // RIM == col_of // RIM, upto - ones, 0.0).astype(jnp.bfloat16)

    for t in range(depth):
        both = split_dot(buf[0, t], prefix_matrix)
        prefix[0, t] = both[:, :lanes]
        total[0, t] = both[:, lanes:]
    tail_sum = split_dot(pack[...].reshape(tiles * SUB, lanes), slot_matrix)

    def slot_pattern(tile, turn):
        order = jnp.minimum(tile * slots + ((slot_of + turn) & (slots - 1)), depth * groups - 1)
        group = (order * 13) >> 6
        return (group & (slots - 1)) * RIM, order - depth * group

    def heads(columns, tile):
        base, t = slot_pattern(tile, slots - 1)
        return take(columns[tile * slots // (depth * slots)], base + 2 * t + (lane & 1))

    for tile in range(tiles):
        own_head[tile] = heads(ecol, tile)
    local[3].wait()

    def rim_tables(part):
        first_tile, last_tile = part
        got_sum = split_dot(got_pack[first_tile:last_tile].reshape((last_tile - first_tile) * SUB, lanes), slot_matrix)
        for tile in range(first_tile, last_tile):
            base, t = slot_pattern(tile, 0)
            columns = got_ecol[tile * slots // (depth * slots)]
            ahead = heads(got_ecol, tile)
            tail = pack[tile]
            left, right = packed_edges(tail, ahead, in_slot)
            depart = take(columns, base + 2 * depth).astype(jnp.int32)
            courant = take(columns, base + 2 * depth + 1)
            index = (slot_of * RIM + (RIM - 1) - depart) & (lanes - 1)
            east_flux_buf[tile] = frac_flux(
                courant, take(right, index), take(left, index), take(tail, index)
            ) - take(tail_sum[tile * SUB : (tile + 1) * SUB], index)
            west = got_pack[tile]
            low_left[tile], low_right[tile] = packed_edges(west, own_head[tile], in_slot)
            low_sum[tile] = got_sum[(tile - first_tile) * SUB : (tile - first_tile + 1) * SUB]
            halo[tile] = jnp.where(in_slot < 2, ahead, west)
            low_cell[tile] = west

    def arrive():
        for copy in rim_copies:
            copy.wait()
        for part in edge_parts:
            rim_tables(part)

    def arrive_rest():
        inner_copy.wait()
        rim_tables(inner_part)

    def finish(t, first, own, flux, east_flux):
        next_flux = roll(jnp.where(lane == 0, east_flux, flux), -1)
        after[t, pl.ds(pl.multiple_of(first + SUB, SUB), SUB), :] = own - (next_flux - flux)

    def near_zonal(group):
        first = pl.multiple_of(group * SUB, SUB)
        span = pl.ds(first, SUB)
        courant = fr_buf[span, :]
        depart = lane - off_buf[span, :] - 1
        in_low = depart < 0
        index = depart & (lanes - 1)
        for t in range(depth):
            order = group * depth + t
            tile, slot = order // slots, lax.rem(order, slots)
            own = buf[0, t, span, :]
            around = take(halo[tile], (lane + RIM * (slot + 1)) & (lanes - 1))
            left, right = edge_pair(own, around, around, lane)
            own_prefix = prefix[0, t, span, :]
            low_index = (depart + RIM * (slot + 1)) & (lanes - 1)

            def pick(table, low_table):
                return jnp.where(in_low, take(low_table[tile], low_index), take(table, index))

            flux = (
                (own_prefix - own)
                - pick(own_prefix, low_sum)
                + frac_flux(courant, pick(right, low_right), pick(left, low_left), pick(own, low_cell))
            )
            east_flux = take(east_flux_buf[tile], jnp.full((SUB, lanes), 0, jnp.int32) + slot * RIM)
            finish(t, first, own, flux, east_flux)

    def is_polar(group):
        return (south_end & (group < POLAR_GROUPS)) | (north_end & (group >= groups - POLAR_GROUPS))

    def full_zonal(group):
        first = pl.multiple_of(group * SUB, SUB)
        span = pl.ds(first, SUB)
        far = jnp.where(is_polar(group), 1, 0)
        off = off_buf[span, :]
        courant = fr_buf[span, :]
        east = got_ecol[group // slots]
        base = lax.rem(group, slots) * RIM
        east_off = take(east, jnp.full((SUB, lanes), 0, jnp.int32) + (base + 2 * depth)).astype(jnp.int32)
        east_courant = take(east, jnp.full((SUB, lanes), 0, jnp.int32) + (base + 2 * depth + 1))
        depart = lane - off - 1 + far * lanes
        in_low = depart < 0
        index = depart & (lanes - 1)
        east_index = (lanes - 1 - east_off + far * lanes) & (lanes - 1)
        for t in range(depth):
            own = buf[0, t, span, :]
            near = buf[far, t, span, :]
            low = lo_buf[t, span, :]
            order = group * depth + t
            beyond = take(got_far[order // slots], (lane + RIM * (lax.rem(order, slots) + 1)) & (lanes - 1))
            ahead = take(east, (lane + (base + 2 * t)) & (lanes - 1))
            ahead = jnp.where(far == 1, own, ahead)
            near_left, near_right = edge_pair(near, low, ahead, lane)
            far_left, far_right = edge_pair(low, beyond, near, lane)
            near_prefix = prefix[far, t, span, :]
            far_total = jnp.where(far == 1, total[far, t, span, :], 0.0)

            def pick(near_table, low_table):
                return jnp.where(in_low, take(low_table, index), take(near_table, index))

            flux = (
                (prefix[0, t, span, :] - own + far_total)
                - pick(near_prefix, suffix[t, span, :])
                + frac_flux(courant, pick(near_right, far_right), pick(near_left, far_left), pick(near, low))
            )
            east_flux = (
                (total[0, t, span, :] + far_total)
                - take(near_prefix, east_index)
                + frac_flux(
                    east_courant, take(near_right, east_index), take(near_left, east_index), take(near, east_index)
                )
            )
            finish(t, first, own, flux, east_flux)

    edge_one = jnp.where(south_end, groups - 1, 0)
    edge_two = jnp.where(north_end, 1, jnp.where(south_end, groups - 2, groups - 1))
    to_south = remote(after.at[:, pl.ds(SUB, 2)], after.at[:, pl.ds(SUB + rows, 2)], 6, lat_dev(-1))
    to_north = remote(after.at[:, pl.ds(SUB + rows - 3, 3)], after.at[:, pl.ds(SUB - 3, 3)], 7, lat_dev(1))
    inner = jnp.where(south_end, FULL_GROUPS, jnp.where(north_end, 2, 1))
    pairs = jnp.where(polar, (groups - FULL_GROUPS) // 2 - 1, groups // 2 - 1)

    def pair(i, carry):
        pl.when(i == 1)(arrive)
        pl.when(i == 2)(arrive_rest)
        near_zonal(jnp.where(i < 2, edge_one, inner + 2 * i - 4))
        near_zonal(jnp.where(i < 2, edge_two, inner + 2 * i - 3))

        @pl.when(i == 1)
        def _():
            pl.when(has_south)(to_south.start)
            pl.when(has_north)(to_north.start)

        return carry

    lax.fori_loop(0, pairs + 2, pair, 0)

    @pl.when(polar)
    def _():
        for copy in polar_copies:
            copy.wait()
        lo_buf[:, full_span, :] = buf[1, :, full_span, :]
        lo_buf[:, polar_span, :] = west_two[:, polar_span, :]
        for t in range(depth):
            both = split_dot(buf[1, t, polar_span, :], prefix_matrix)
            prefix[1, t, polar_span, :] = both[:, :lanes]
            total[1, t, polar_span, :] = both[:, lanes:]
            suffix[t, full_span, :] = split_dot(lo_buf[t, full_span, :], suffix_matrix)

        def full_pair(i, carry):
            full_zonal(full_row // SUB + 2 * i)
            full_zonal(full_row // SUB + 2 * i + 1)
            return carry

        lax.fori_loop(0, FULL_GROUPS // 2, full_pair, 0)

    def merid(t, first, count):
        at = first + SUB
        edge_buf[t, at - 1 : at + count + 1, :] = wide_weight * (
            after[t, at - 2 : at + count, :] + after[t, at - 1 : at + count + 1, :]
        ) - narrow_weight * (after[t, at - 3 : at + count - 1, :] + after[t, at : at + count + 2, :])
        flux_buf[t, first : first + count + 1, :] = frac_flux(
            cn_buf[first : first + count + 1, :],
            edge_buf[t, at : at + count + 1, :],
            edge_buf[t, at - 1 : at + count, :],
            after[t, at - 1 : at + count, :],
        )
        done[t, first : first + count, :] = after[t, at : at + count, :] - (
            flux_buf[t, first + 1 : first + count + 1, :] - flux_buf[t, first : first + count, :]
        )

    def merid_inner(t, carry):
        merid(t, SUB, rows - 2 * SUB)
        return carry

    lax.fori_loop(0, depth, merid_inner, 0)

    @pl.when(has_south)
    def _():
        courant_copy.wait_send()
        to_south.wait_send()
        to_north.wait_recv()

    @pl.when(has_north)
    def _():
        to_north.wait_send()
        to_south.wait_recv()
        courant_copy.wait_recv()

    @pl.when(south_end)
    def _():
        after[:, 0:SUB, :] = jnp.zeros((depth, SUB, lanes), jnp.float32)
        cn_buf[0:1, :] = jnp.zeros((1, lanes), jnp.float32)

    @pl.when(north_end)
    def _():
        after[:, SUB + rows :, :] = jnp.zeros((depth, SUB, lanes), jnp.float32)
        cn_buf[rows:, :] = jnp.zeros((SUB, lanes), jnp.float32)

    def merid_rim(t, carry):
        merid(t, 0, SUB)
        merid(t, rows - SUB, SUB)
        return carry

    lax.fori_loop(0, depth, merid_rim, 0)


def store_kernel(done, out, sem):
    copy = pltpu.make_async_copy(done, out, sem)
    copy.start()
    copy.wait()


def on_device(sizes, tracers, offsets, fraction, courant_north):
    tracer_count, level_count, rows, lanes = tracers.shape
    depth = tracer_count * level_count
    f32 = jnp.float32
    groups = rows // SUB
    slots = lanes // RIM
    tiles = -(-(depth * groups) // slots)
    column_tiles = -(-groups // slots)
    anywhere = pl.BlockSpec(memory_space=pl.ANY)
    vmem = pl.BlockSpec(memory_space=pltpu.VMEM)
    packed = pltpu.VMEM((tiles, SUB, lanes), f32)
    columns = pltpu.VMEM((column_tiles, SUB, lanes), f32)
    block = pltpu.VMEM((depth, rows, lanes), f32)
    two_blocks = pltpu.VMEM((2, depth, rows, lanes), f32)
    done = pl.pallas_call(
        functools.partial(step_kernel, sizes),
        out_shape=pltpu.VMEM((depth, rows, lanes), f32),
        in_specs=[pl.BlockSpec(memory_space=pltpu.HBM)] * 4,
        out_specs=vmem,
        scratch_shapes=[
            pltpu.VMEM((depth, rows + 2 * SUB, lanes), f32),
            pltpu.VMEM((rows + SUB, lanes), f32),
            pltpu.VMEM((depth, rows + 2 * SUB, lanes), f32),
            pltpu.VMEM((depth, rows + SUB, lanes), f32),
            two_blocks,
            pltpu.VMEM((rows, lanes), jnp.int32),
            pltpu.VMEM((rows, lanes), f32),
            block,
            packed, columns, packed, columns, packed,
            block, two_blocks, two_blocks, block,
            packed, packed, packed, packed, packed, packed, packed,
            pltpu.SemaphoreType.DMA((4,)),
            pltpu.SemaphoreType.DMA((10,)),
            pltpu.SemaphoreType.DMA((10,)),
        ],
        compiler_params=pltpu.CompilerParams(collective_id=0, has_side_effects=True, vmem_limit_bytes=66_747_392),
    )(tracers.reshape(depth, rows, lanes), offsets, fraction, courant_north)
    advected = pl.pallas_call(
        store_kernel,
        out_shape=jax.ShapeDtypeStruct((depth, rows, lanes), f32),
        in_specs=[vmem],
        out_specs=anywhere,
        scratch_shapes=[pltpu.SemaphoreType.DMA],
        compiler_params=pltpu.CompilerParams(vmem_limit_bytes=8 << 20),
    )(done)
    return advected.reshape(tracers.shape)


def solution(mesh):
    placed = (P(None, None, "lat", "lon"), P("lat", "lon"), P("lat", "lon"), P("lat", "lon"))
    return jax.shard_map(
        functools.partial(on_device, (mesh.shape["lat"], mesh.shape["lon"])),
        mesh=mesh,
        in_specs=placed,
        out_specs=P(None, None, "lat", "lon"),
        check_vma=False,
    )
```

```python
import functools

import jax
import jax.numpy as jnp
from jax import lax
from jax.experimental import pallas as pl
from jax.experimental.pallas import tpu as pltpu
from jax.sharding import PartitionSpec as P

wide_weight = 7.0 / 12.0
narrow_weight = 1.0 / 12.0
MESH = pl.DeviceIdType.MESH
SUB = 8
RIM = 16
POLAR_GROUPS = 3
FULL_GROUPS = 6


def take(table, index):
    return jnp.take_along_axis(table, index, axis=1, mode="promise_in_bounds")


def split_dot(value, matrix):
    high = value.astype(jnp.bfloat16)
    low = (value - high.astype(jnp.float32)).astype(jnp.bfloat16)
    return jnp.dot(high, matrix, preferred_element_type=jnp.float32) + jnp.dot(
        low, matrix, preferred_element_type=jnp.float32
    )


def frac_flux(courant, right, left, centre):
    jump = right - left
    curve = 6.0 * (centre - 0.5 * (left + right))
    return courant * (right - 0.5 * courant * (jump - (1.0 - 2.0 / 3.0 * courant) * curve))


def roll(value, steps):
    steps = steps % value.shape[-1]
    return value if steps == 0 else pltpu.roll(value, steps, 1)


def edge_pair(cells, west, east, lane):
    last = cells.shape[-1]
    minus_two = roll(jnp.where(lane >= last - 2, west, cells), 2)
    minus_one = roll(jnp.where(lane >= last - 1, west, cells), 1)
    plus_one = roll(jnp.where(lane < 1, east, cells), -1)
    plus_two = roll(jnp.where(lane < 2, east, cells), -2)
    left = wide_weight * (minus_one + cells) - narrow_weight * (minus_two + plus_one)
    right = wide_weight * (cells + plus_one) - narrow_weight * (minus_one + plus_two)
    return left, right


def packed_edges(cells, ahead, in_slot):
    minus_one = roll(cells, 1)
    minus_two = roll(cells, 2)
    plus_one = roll(jnp.where(in_slot < 1, ahead, cells), -1)
    plus_two = roll(jnp.where(in_slot < 2, ahead, cells), -2)
    left = wide_weight * (minus_one + cells) - narrow_weight * (minus_two + plus_one)
    right = wide_weight * (cells + plus_one) - narrow_weight * (minus_one + plus_two)
    return left, right


def step_kernel(
    sizes, tr, off_in, fr_in, cn_in, done,
    after, cn_buf, edge_buf, flux_buf, buf, off_buf, fr_buf, west_two, pack, ecol, got_pack, got_ecol, got_far,
    lo_buf, prefix, total, suffix, own_head, halo, east_flux_buf, low_left, low_right, low_sum, low_cell,
    local_sem, send_sem, recv_sem,
):
    lat_count, lon_count = sizes
    depth, rows, lanes = tr.shape
    groups = rows // SUB
    slots = lanes // RIM
    tiles = pack.shape[0]
    lat, lon = lax.axis_index("lat"), lax.axis_index("lon")
    south_end = lat == 0
    north_end = lat == lat_count - 1
    polar = south_end | north_end
    has_south = lat > 0
    has_north = lat < lat_count - 1

    local = [
        pltpu.make_async_copy(tr, buf.at[0], local_sem.at[0]),
        pltpu.make_async_copy(off_in, off_buf, local_sem.at[1]),
        pltpu.make_async_copy(fr_in, fr_buf, local_sem.at[2]),
        pltpu.make_async_copy(cn_in, cn_buf.at[pl.ds(0, rows)], local_sem.at[3]),
    ]
    for copy in local:
        copy.start()

    def lon_dev(steps):
        return {"lat": lat, "lon": lax.rem(lon + steps + lon_count, lon_count)}

    def lat_dev(steps):
        return {"lat": lax.rem(lat + steps + lat_count, lat_count), "lon": lon}

    barrier = pltpu.get_barrier_semaphore()

    def greet(device):
        pl.semaphore_signal(barrier, inc=1, device_id=device, device_id_type=MESH)

    greet(lon_dev(1))
    greet(lon_dev(-1))
    pl.when(has_south)(lambda: greet(lat_dev(-1)))
    pl.when(has_north)(lambda: greet(lat_dev(1)))

    @pl.when(polar)
    def _():
        for steps in (2, -2, 3, -3):
            greet(lon_dev(steps))

    lane = lax.broadcasted_iota(jnp.int32, (SUB, lanes), 1)
    slot_of = lane // RIM
    in_slot = lane & (RIM - 1)

    for copy in local[:3]:
        copy.wait()

    edge_parts = ((0, 2), (tiles - 2, tiles))
    inner_part = (2, tiles - 2)

    def pack_rims(part):
        for tile in range(*part):
            packed = jnp.zeros((SUB, lanes), jnp.float32)
            for slot in range(slots):
                group, t = divmod(tile * slots + slot, depth)
                if group >= groups:
                    break
                cells = buf[0, t, group * SUB : (group + 1) * SUB, :]
                packed = jnp.where(slot_of == slot, roll(cells, RIM * (slot + 1)), packed)
            pack[tile] = packed

    for part in edge_parts:
        pack_rims(part)
    for tile in range(ecol.shape[0]):
        packed = jnp.zeros((SUB, lanes), jnp.float32)
        for slot in range(slots):
            group = tile * slots + slot
            if group >= groups:
                break
            span = slice(group * SUB, (group + 1) * SUB)
            base = slot * RIM
            for t in range(depth):
                at = base + 2 * t
                packed = jnp.where((lane >= at) & (lane < at + 2), roll(buf[0, t, span, :], at), packed)
            at = base + 2 * depth
            packed = jnp.where(lane == at, roll(off_buf[span, :].astype(jnp.float32), at), packed)
            packed = jnp.where(lane == at + 1, roll(fr_buf[span, :], at + 1), packed)
        ecol[tile] = packed

    pl.semaphore_wait(barrier, jnp.where(polar, 7, 4))

    def remote(source, target, index, device):
        return pltpu.make_async_remote_copy(
            src_ref=source, dst_ref=target, send_sem=send_sem.at[index], recv_sem=recv_sem.at[index],
            device_id=device, device_id_type=MESH,
        )

    full_row = jnp.where(south_end, 0, rows - FULL_GROUPS * SUB)
    full_span = pl.ds(pl.multiple_of(full_row, SUB), FULL_GROUPS * SUB)
    polar_row = jnp.where(south_end, 0, rows - POLAR_GROUPS * SUB)
    polar_span = pl.ds(pl.multiple_of(polar_row, SUB), POLAR_GROUPS * SUB)
    far_span = pl.ds(jnp.where(south_end, 0, tiles - 3), 3)
    def rim_copy(part, index):
        span = pl.ds(part[0], part[1] - part[0])
        return remote(pack.at[span], got_pack.at[span], index, lon_dev(1))

    rim_copies = [rim_copy(edge_parts[0], 0), rim_copy(edge_parts[1], 8), remote(ecol, got_ecol, 1, lon_dev(-1))]
    inner_copy = rim_copy(inner_part, 9)
    for copy in rim_copies:
        copy.start()
    pack_rims(inner_part)
    inner_copy.start()
    polar_copies = [
        remote(tr.at[:, full_span], buf.at[1, :, full_span], 3, lon_dev(1)),
        remote(tr.at[:, polar_span], west_two.at[:, polar_span], 4, lon_dev(2)),
        remote(pack.at[far_span], got_far.at[far_span], 5, lon_dev(3)),
    ]

    @pl.when(polar)
    def _():
        for copy in polar_copies:
            copy.start()

    courant_copy = remote(cn_in.at[pl.ds(0, SUB)], cn_buf.at[pl.ds(rows, SUB)], 2, lat_dev(-1))
    pl.when(has_south)(courant_copy.start)

    row_of = lax.broadcasted_iota(jnp.int32, (lanes, lanes), 0)
    col_of = lax.broadcasted_iota(jnp.int32, (lanes, lanes), 1)
    ones = jnp.ones((lanes, lanes), jnp.float32)
    upto = (row_of <= col_of).astype(jnp.float32)
    prefix_matrix = jnp.concatenate([upto, ones], axis=1).astype(jnp.bfloat16)
    suffix_matrix = (upto - ones).astype(jnp.bfloat16)
    slot_matrix = jnp.where(row_of // RIM == col_of // RIM, upto - ones, 0.0).astype(jnp.bfloat16)

    for t in range(depth):
        both = split_dot(buf[0, t], prefix_matrix)
        prefix[0, t] = both[:, :lanes]
        total[0, t] = both[:, lanes:]
    tail_sum = split_dot(pack[...].reshape(tiles * SUB, lanes), slot_matrix)

    def slot_pattern(tile, turn):
        order = jnp.minimum(tile * slots + ((slot_of + turn) & (slots - 1)), depth * groups - 1)
        group = (order * 13) >> 6
        return (group & (slots - 1)) * RIM, order - depth * group

    def heads(columns, tile):
        base, t = slot_pattern(tile, slots - 1)
        return take(columns[tile * slots // (depth * slots)], base + 2 * t + (lane & 1))

    for tile in range(tiles):
        own_head[tile] = heads(ecol, tile)
    local[3].wait()

    def rim_tables(part):
        first_tile, last_tile = part
        got_sum = split_dot(got_pack[first_tile:last_tile].reshape((last_tile - first_tile) * SUB, lanes), slot_matrix)
        for tile in range(first_tile, last_tile):
            base, t = slot_pattern(tile, 0)
            columns = got_ecol[tile * slots // (depth * slots)]
            ahead = heads(got_ecol, tile)
            tail = pack[tile]
            left, right = packed_edges(tail, ahead, in_slot)
            depart = take(columns, base + 2 * depth).astype(jnp.int32)
            courant = take(columns, base + 2 * depth + 1)
            index = (slot_of * RIM + (RIM - 1) - depart) & (lanes - 1)
            east_flux_buf[tile] = frac_flux(
                courant, take(right, index), take(left, index), take(tail, index)
            ) - take(tail_sum[tile * SUB : (tile + 1) * SUB], index)
            west = got_pack[tile]
            low_left[tile], low_right[tile] = packed_edges(west, own_head[tile], in_slot)
            low_sum[tile] = got_sum[(tile - first_tile) * SUB : (tile - first_tile + 1) * SUB]
            halo[tile] = jnp.where(in_slot < 2, ahead, west)
            low_cell[tile] = west

    def arrive():
        for copy in rim_copies:
            copy.wait()
        for part in edge_parts:
            rim_tables(part)

    def arrive_rest():
        inner_copy.wait()
        rim_tables(inner_part)

    def finish(t, first, own, flux, east_flux):
        next_flux = roll(jnp.where(lane == 0, east_flux, flux), -1)
        after[t, pl.ds(pl.multiple_of(first + SUB, SUB), SUB), :] = own - (next_flux - flux)

    def near_zonal(group):
        first = pl.multiple_of(group * SUB, SUB)
        span = pl.ds(first, SUB)
        courant = fr_buf[span, :]
        depart = lane - off_buf[span, :] - 1
        in_low = depart < 0
        index = depart & (lanes - 1)
        for t in range(depth):
            order = group * depth + t
            tile, slot = order // slots, lax.rem(order, slots)
            own = buf[0, t, span, :]
            around = take(halo[tile], (lane + RIM * (slot + 1)) & (lanes - 1))
            left, right = edge_pair(own, around, around, lane)
            own_prefix = prefix[0, t, span, :]
            low_index = (depart + RIM * (slot + 1)) & (lanes - 1)

            def pick(table, low_table):
                return jnp.where(in_low, take(low_table[tile], low_index), take(table, index))

            flux = (
                (own_prefix - own)
                - pick(own_prefix, low_sum)
                + frac_flux(courant, pick(right, low_right), pick(left, low_left), pick(own, low_cell))
            )
            east_flux = take(east_flux_buf[tile], jnp.full((SUB, lanes), 0, jnp.int32) + slot * RIM)
            finish(t, first, own, flux, east_flux)

    def is_polar(group):
        return (south_end & (group < POLAR_GROUPS)) | (north_end & (group >= groups - POLAR_GROUPS))

    def full_zonal(group):
        first = pl.multiple_of(group * SUB, SUB)
        span = pl.ds(first, SUB)
        far = jnp.where(is_polar(group), 1, 0)
        off = off_buf[span, :]
        courant = fr_buf[span, :]
        east = got_ecol[group // slots]
        base = lax.rem(group, slots) * RIM
        east_off = take(east, jnp.full((SUB, lanes), 0, jnp.int32) + (base + 2 * depth)).astype(jnp.int32)
        east_courant = take(east, jnp.full((SUB, lanes), 0, jnp.int32) + (base + 2 * depth + 1))
        depart = lane - off - 1 + far * lanes
        in_low = depart < 0
        index = depart & (lanes - 1)
        east_index = (lanes - 1 - east_off + far * lanes) & (lanes - 1)
        for t in range(depth):
            own = buf[0, t, span, :]
            near = buf[far, t, span, :]
            low = lo_buf[t, span, :]
            order = group * depth + t
            beyond = take(got_far[order // slots], (lane + RIM * (lax.rem(order, slots) + 1)) & (lanes - 1))
            ahead = take(east, (lane + (base + 2 * t)) & (lanes - 1))
            ahead = jnp.where(far == 1, own, ahead)
            near_left, near_right = edge_pair(near, low, ahead, lane)
            far_left, far_right = edge_pair(low, beyond, near, lane)
            near_prefix = prefix[far, t, span, :]
            far_total = jnp.where(far == 1, total[far, t, span, :], 0.0)

            def pick(near_table, low_table):
                return jnp.where(in_low, take(low_table, index), take(near_table, index))

            flux = (
                (prefix[0, t, span, :] - own + far_total)
                - pick(near_prefix, suffix[t, span, :])
                + frac_flux(courant, pick(near_right, far_right), pick(near_left, far_left), pick(near, low))
            )
            east_flux = (
                (total[0, t, span, :] + far_total)
                - take(near_prefix, east_index)
                + frac_flux(
                    east_courant, take(near_right, east_index), take(near_left, east_index), take(near, east_index)
                )
            )
            finish(t, first, own, flux, east_flux)

    edge_one = jnp.where(south_end, groups - 1, 0)
    edge_two = jnp.where(north_end, 1, jnp.where(south_end, groups - 2, groups - 1))
    to_south = remote(after.at[:, pl.ds(SUB, SUB)], after.at[:, pl.ds(SUB + rows, SUB)], 6, lat_dev(-1))
    to_north = remote(after.at[:, pl.ds(rows, SUB)], after.at[:, pl.ds(0, SUB)], 7, lat_dev(1))
    inner = jnp.where(south_end, FULL_GROUPS, jnp.where(north_end, 2, 1))
    pairs = jnp.where(polar, (groups - FULL_GROUPS) // 2 - 1, groups // 2 - 1)

    def pair(i, carry):
        pl.when(i == 1)(arrive)
        pl.when(i == 2)(arrive_rest)
        near_zonal(jnp.where(i < 2, edge_one, inner + 2 * i - 4))
        near_zonal(jnp.where(i < 2, edge_two, inner + 2 * i - 3))

        @pl.when(i == 1)
        def _():
            pl.when(has_south)(to_south.start)
            pl.when(has_north)(to_north.start)

        return carry

    lax.fori_loop(0, pairs + 2, pair, 0)

    @pl.when(polar)
    def _():
        for copy in polar_copies:
            copy.wait()
        lo_buf[:, full_span, :] = buf[1, :, full_span, :]
        lo_buf[:, polar_span, :] = west_two[:, polar_span, :]
        for t in range(depth):
            both = split_dot(buf[1, t, polar_span, :], prefix_matrix)
            prefix[1, t, polar_span, :] = both[:, :lanes]
            total[1, t, polar_span, :] = both[:, lanes:]
            suffix[t, full_span, :] = split_dot(lo_buf[t, full_span, :], suffix_matrix)

        def full_pair(i, carry):
            full_zonal(full_row // SUB + 2 * i)
            full_zonal(full_row // SUB + 2 * i + 1)
            return carry

        lax.fori_loop(0, FULL_GROUPS // 2, full_pair, 0)

    def merid(t, first, count):
        at = first + SUB
        edge_buf[t, at - 1 : at + count + 1, :] = wide_weight * (
            after[t, at - 2 : at + count, :] + after[t, at - 1 : at + count + 1, :]
        ) - narrow_weight * (after[t, at - 3 : at + count - 1, :] + after[t, at : at + count + 2, :])
        flux_buf[t, first : first + count + 1, :] = frac_flux(
            cn_buf[first : first + count + 1, :],
            edge_buf[t, at : at + count + 1, :],
            edge_buf[t, at - 1 : at + count, :],
            after[t, at - 1 : at + count, :],
        )
        done[t, first : first + count, :] = after[t, at : at + count, :] - (
            flux_buf[t, first + 1 : first + count + 1, :] - flux_buf[t, first : first + count, :]
        )

    def merid_inner(t, carry):
        merid(t, SUB, rows - 2 * SUB)
        return carry

    lax.fori_loop(0, depth, merid_inner, 0)

    @pl.when(has_south)
    def _():
        courant_copy.wait_send()
        to_south.wait_send()
        to_north.wait_recv()

    @pl.when(has_north)
    def _():
        to_north.wait_send()
        to_south.wait_recv()
        courant_copy.wait_recv()

    @pl.when(south_end)
    def _():
        after[:, 0:SUB, :] = jnp.zeros((depth, SUB, lanes), jnp.float32)
        cn_buf[0:1, :] = jnp.zeros((1, lanes), jnp.float32)

    @pl.when(north_end)
    def _():
        after[:, SUB + rows :, :] = jnp.zeros((depth, SUB, lanes), jnp.float32)
        cn_buf[rows:, :] = jnp.zeros((SUB, lanes), jnp.float32)

    def merid_rim(t, carry):
        merid(t, 0, SUB)
        merid(t, rows - SUB, SUB)
        return carry

    lax.fori_loop(0, depth, merid_rim, 0)


def store_kernel(done, out, sem):
    copy = pltpu.make_async_copy(done, out, sem)
    copy.start()
    copy.wait()


def on_device(sizes, tracers, offsets, fraction, courant_north):
    tracer_count, level_count, rows, lanes = tracers.shape
    depth = tracer_count * level_count
    f32 = jnp.float32
    groups = rows // SUB
    slots = lanes // RIM
    tiles = -(-(depth * groups) // slots)
    column_tiles = -(-groups // slots)
    anywhere = pl.BlockSpec(memory_space=pl.ANY)
    vmem = pl.BlockSpec(memory_space=pltpu.VMEM)
    packed = pltpu.VMEM((tiles, SUB, lanes), f32)
    columns = pltpu.VMEM((column_tiles, SUB, lanes), f32)
    block = pltpu.VMEM((depth, rows, lanes), f32)
    two_blocks = pltpu.VMEM((2, depth, rows, lanes), f32)
    done = pl.pallas_call(
        functools.partial(step_kernel, sizes),
        out_shape=pltpu.VMEM((depth, rows, lanes), f32),
        in_specs=[pl.BlockSpec(memory_space=pltpu.HBM)] * 4,
        out_specs=vmem,
        scratch_shapes=[
            pltpu.VMEM((depth, rows + 2 * SUB, lanes), f32),
            pltpu.VMEM((rows + SUB, lanes), f32),
            pltpu.VMEM((depth, rows + 2 * SUB, lanes), f32),
            pltpu.VMEM((depth, rows + SUB, lanes), f32),
            two_blocks,
            pltpu.VMEM((rows, lanes), jnp.int32),
            pltpu.VMEM((rows, lanes), f32),
            block,
            packed, columns, packed, columns, packed,
            block, two_blocks, two_blocks, block,
            packed, packed, packed, packed, packed, packed, packed,
            pltpu.SemaphoreType.DMA((4,)),
            pltpu.SemaphoreType.DMA((10,)),
            pltpu.SemaphoreType.DMA((10,)),
        ],
        compiler_params=pltpu.CompilerParams(collective_id=0, has_side_effects=True, vmem_limit_bytes=66_747_392),
    )(tracers.reshape(depth, rows, lanes), offsets, fraction, courant_north)
    advected = pl.pallas_call(
        store_kernel,
        out_shape=jax.ShapeDtypeStruct((depth, rows, lanes), f32),
        in_specs=[vmem],
        out_specs=anywhere,
        scratch_shapes=[pltpu.SemaphoreType.DMA],
        compiler_params=pltpu.CompilerParams(vmem_limit_bytes=8 << 20),
    )(done)
    return advected.reshape(tracers.shape)


def solution(mesh):
    placed = (P(None, None, "lat", "lon"), P("lat", "lon"), P("lat", "lon"), P("lat", "lon"))
    return jax.shard_map(
        functools.partial(on_device, (mesh.shape["lat"], mesh.shape["lon"])),
        mesh=mesh,
        in_specs=placed,
        out_specs=P(None, None, "lat", "lon"),
        check_vma=False,
    )
```

```python
import functools

import jax
import jax.numpy as jnp
from jax import lax
from jax.experimental import pallas as pl
from jax.experimental.pallas import tpu as pltpu
from jax.sharding import PartitionSpec as P

wide_weight = 7.0 / 12.0
narrow_weight = 1.0 / 12.0
MESH = pl.DeviceIdType.MESH
SUB = 8
RIM = 16
POLAR_GROUPS = 3
FULL_GROUPS = 6


def take(table, index):
    return jnp.take_along_axis(table, index, axis=1, mode="promise_in_bounds")


def split_dot(value, matrix):
    high = value.astype(jnp.bfloat16)
    low = (value - high.astype(jnp.float32)).astype(jnp.bfloat16)
    return jnp.dot(high, matrix, preferred_element_type=jnp.float32) + jnp.dot(
        low, matrix, preferred_element_type=jnp.float32
    )


def frac_flux(courant, right, left, centre):
    jump = right - left
    curve = 6.0 * (centre - 0.5 * (left + right))
    return courant * (right - 0.5 * courant * (jump - (1.0 - 2.0 / 3.0 * courant) * curve))


def roll(value, steps):
    steps = steps % value.shape[-1]
    return value if steps == 0 else pltpu.roll(value, steps, 1)


def edge_pair(cells, west, east, lane):
    last = cells.shape[-1]
    minus_two = roll(jnp.where(lane >= last - 2, west, cells), 2)
    minus_one = roll(jnp.where(lane >= last - 1, west, cells), 1)
    plus_one = roll(jnp.where(lane < 1, east, cells), -1)
    plus_two = roll(jnp.where(lane < 2, east, cells), -2)
    left = wide_weight * (minus_one + cells) - narrow_weight * (minus_two + plus_one)
    right = wide_weight * (cells + plus_one) - narrow_weight * (minus_one + plus_two)
    return left, right


def packed_edges(cells, ahead, in_slot):
    minus_one = roll(cells, 1)
    minus_two = roll(cells, 2)
    plus_one = roll(jnp.where(in_slot < 1, ahead, cells), -1)
    plus_two = roll(jnp.where(in_slot < 2, ahead, cells), -2)
    left = wide_weight * (minus_one + cells) - narrow_weight * (minus_two + plus_one)
    right = wide_weight * (cells + plus_one) - narrow_weight * (minus_one + plus_two)
    return left, right


def step_kernel(
    sizes, tr, off_in, fr_in, cn_in, done,
    after, cn_buf, edge_buf, flux_buf, buf, off_buf, fr_buf, west_two, pack, ecol, got_pack, got_ecol, got_far,
    lo_buf, prefix, total, suffix, own_head, halo, east_flux_buf, low_left, low_right, low_sum, low_cell,
    local_sem, send_sem, recv_sem,
):
    lat_count, lon_count = sizes
    depth, rows, lanes = tr.shape
    groups = rows // SUB
    slots = lanes // RIM
    tiles = pack.shape[0]
    lat, lon = lax.axis_index("lat"), lax.axis_index("lon")
    south_end = lat == 0
    north_end = lat == lat_count - 1
    polar = south_end | north_end
    has_south = lat > 0
    has_north = lat < lat_count - 1

    local = [
        pltpu.make_async_copy(tr, buf.at[0], local_sem.at[0]),
        pltpu.make_async_copy(off_in, off_buf, local_sem.at[1]),
        pltpu.make_async_copy(fr_in, fr_buf, local_sem.at[2]),
        pltpu.make_async_copy(cn_in, cn_buf.at[pl.ds(0, rows)], local_sem.at[3]),
    ]
    for copy in local:
        copy.start()

    def lon_dev(steps):
        return {"lat": lat, "lon": lax.rem(lon + steps + lon_count, lon_count)}

    def lat_dev(steps):
        return {"lat": lax.rem(lat + steps + lat_count, lat_count), "lon": lon}

    barrier = pltpu.get_barrier_semaphore()

    def greet(device):
        pl.semaphore_signal(barrier, inc=1, device_id=device, device_id_type=MESH)

    greet(lon_dev(1))
    greet(lon_dev(-1))
    pl.when(has_south)(lambda: greet(lat_dev(-1)))
    pl.when(has_north)(lambda: greet(lat_dev(1)))

    @pl.when(polar)
    def _():
        for steps in (2, -2, 3, -3):
            greet(lon_dev(steps))

    lane = lax.broadcasted_iota(jnp.int32, (SUB, lanes), 1)
    slot_of = lane // RIM
    in_slot = lane & (RIM - 1)

    for copy in local[:3]:
        copy.wait()

    for tile in range(tiles):
        packed = jnp.zeros((SUB, lanes), jnp.float32)
        for slot in range(slots):
            group, t = divmod(tile * slots + slot, depth)
            if group >= groups:
                break
            cells = buf[0, t, group * SUB : (group + 1) * SUB, :]
            packed = jnp.where(slot_of == slot, roll(cells, RIM * (slot + 1)), packed)
        pack[tile] = packed
    for tile in range(ecol.shape[0]):
        packed = jnp.zeros((SUB, lanes), jnp.float32)
        for slot in range(slots):
            group = tile * slots + slot
            if group >= groups:
                break
            span = slice(group * SUB, (group + 1) * SUB)
            base = slot * RIM
            for t in range(depth):
                at = base + 2 * t
                packed = jnp.where((lane >= at) & (lane < at + 2), roll(buf[0, t, span, :], at), packed)
            at = base + 2 * depth
            packed = jnp.where(lane == at, roll(off_buf[span, :].astype(jnp.float32), at), packed)
            packed = jnp.where(lane == at + 1, roll(fr_buf[span, :], at + 1), packed)
        ecol[tile] = packed

    pl.semaphore_wait(barrier, jnp.where(polar, 7, 4))

    def remote(source, target, index, device):
        return pltpu.make_async_remote_copy(
            src_ref=source, dst_ref=target, send_sem=send_sem.at[index], recv_sem=recv_sem.at[index],
            device_id=device, device_id_type=MESH,
        )

    full_row = jnp.where(south_end, 0, rows - FULL_GROUPS * SUB)
    full_span = pl.ds(pl.multiple_of(full_row, SUB), FULL_GROUPS * SUB)
    polar_row = jnp.where(south_end, 0, rows - POLAR_GROUPS * SUB)
    polar_span = pl.ds(pl.multiple_of(polar_row, SUB), POLAR_GROUPS * SUB)
    far_span = pl.ds(jnp.where(south_end, 0, tiles - 3), 3)
    edge_parts = ((0, 2), (tiles - 2, tiles))
    inner_part = (2, tiles - 2)

    def rim_copy(part, index):
        span = pl.ds(part[0], part[1] - part[0])
        return remote(pack.at[span], got_pack.at[span], index, lon_dev(1))

    rim_copies = [rim_copy(edge_parts[0], 0), rim_copy(edge_parts[1], 8), remote(ecol, got_ecol, 1, lon_dev(-1))]
    inner_copy = rim_copy(inner_part, 9)
    for copy in rim_copies:
        copy.start()
    inner_copy.start()
    polar_copies = [
        remote(tr.at[:, full_span], buf.at[1, :, full_span], 3, lon_dev(1)),
        remote(tr.at[:, polar_span], west_two.at[:, polar_span], 4, lon_dev(2)),
        remote(pack.at[far_span], got_far.at[far_span], 5, lon_dev(3)),
    ]

    @pl.when(polar)
    def _():
        for copy in polar_copies:
            copy.start()

    courant_copy = remote(cn_in.at[pl.ds(0, SUB)], cn_buf.at[pl.ds(rows, SUB)], 2, lat_dev(-1))
    pl.when(has_south)(courant_copy.start)

    row_of = lax.broadcasted_iota(jnp.int32, (lanes, lanes), 0)
    col_of = lax.broadcasted_iota(jnp.int32, (lanes, lanes), 1)
    ones = jnp.ones((lanes, lanes), jnp.float32)
    upto = (row_of <= col_of).astype(jnp.float32)
    prefix_matrix = jnp.concatenate([upto, ones], axis=1).astype(jnp.bfloat16)
    suffix_matrix = (upto - ones).astype(jnp.bfloat16)
    slot_matrix = jnp.where(row_of // RIM == col_of // RIM, upto - ones, 0.0).astype(jnp.bfloat16)

    for t in range(depth):
        both = split_dot(buf[0, t], prefix_matrix)
        prefix[0, t] = both[:, :lanes]
        total[0, t] = both[:, lanes:]
    tail_sum = split_dot(pack[...].reshape(tiles * SUB, lanes), slot_matrix)

    def slot_pattern(tile, turn):
        order = jnp.minimum(tile * slots + ((slot_of + turn) & (slots - 1)), depth * groups - 1)
        group = (order * 13) >> 6
        return (group & (slots - 1)) * RIM, order - depth * group

    def heads(columns, tile):
        base, t = slot_pattern(tile, slots - 1)
        return take(columns[tile * slots // (depth * slots)], base + 2 * t + (lane & 1))

    for tile in range(tiles):
        own_head[tile] = heads(ecol, tile)
    local[3].wait()

    def rim_tables(part):
        first_tile, last_tile = part
        got_sum = split_dot(got_pack[first_tile:last_tile].reshape((last_tile - first_tile) * SUB, lanes), slot_matrix)
        for tile in range(first_tile, last_tile):
            base, t = slot_pattern(tile, 0)
            columns = got_ecol[tile * slots // (depth * slots)]
            ahead = heads(got_ecol, tile)
            tail = pack[tile]
            left, right = packed_edges(tail, ahead, in_slot)
            depart = take(columns, base + 2 * depth).astype(jnp.int32)
            courant = take(columns, base + 2 * depth + 1)
            index = (slot_of * RIM + (RIM - 1) - depart) & (lanes - 1)
            east_flux_buf[tile] = frac_flux(
                courant, take(right, index), take(left, index), take(tail, index)
            ) - take(tail_sum[tile * SUB : (tile + 1) * SUB], index)
            west = got_pack[tile]
            low_left[tile], low_right[tile] = packed_edges(west, own_head[tile], in_slot)
            low_sum[tile] = got_sum[(tile - first_tile) * SUB : (tile - first_tile + 1) * SUB]
            halo[tile] = jnp.where(in_slot < 2, ahead, west)
            low_cell[tile] = west

    def arrive():
        for copy in rim_copies:
            copy.wait()
        for part in edge_parts:
            rim_tables(part)

    def arrive_rest():
        inner_copy.wait()
        rim_tables(inner_part)

    def finish(t, first, own, flux, east_flux):
        next_flux = roll(jnp.where(lane == 0, east_flux, flux), -1)
        after[t, pl.ds(pl.multiple_of(first + SUB, SUB), SUB), :] = own - (next_flux - flux)

    def near_zonal(group):
        first = pl.multiple_of(group * SUB, SUB)
        span = pl.ds(first, SUB)
        courant = fr_buf[span, :]
        depart = lane - off_buf[span, :] - 1
        in_low = depart < 0
        index = depart & (lanes - 1)
        for t in range(depth):
            order = group * depth + t
            tile, slot = order // slots, lax.rem(order, slots)
            own = buf[0, t, span, :]
            around = take(halo[tile], (lane + RIM * (slot + 1)) & (lanes - 1))
            left, right = edge_pair(own, around, around, lane)
            own_prefix = prefix[0, t, span, :]
            low_index = (depart + RIM * (slot + 1)) & (lanes - 1)

            def pick(table, low_table):
                return jnp.where(in_low, take(low_table[tile], low_index), take(table, index))

            flux = (
                (own_prefix - own)
                - pick(own_prefix, low_sum)
                + frac_flux(courant, pick(right, low_right), pick(left, low_left), pick(own, low_cell))
            )
            east_flux = take(east_flux_buf[tile], jnp.full((SUB, lanes), 0, jnp.int32) + slot * RIM)
            finish(t, first, own, flux, east_flux)

    def is_polar(group):
        return (south_end & (group < POLAR_GROUPS)) | (north_end & (group >= groups - POLAR_GROUPS))

    def full_zonal(group):
        first = pl.multiple_of(group * SUB, SUB)
        span = pl.ds(first, SUB)
        far = jnp.where(is_polar(group), 1, 0)
        off = off_buf[span, :]
        courant = fr_buf[span, :]
        east = got_ecol[group // slots]
        base = lax.rem(group, slots) * RIM
        east_off = take(east, jnp.full((SUB, lanes), 0, jnp.int32) + (base + 2 * depth)).astype(jnp.int32)
        east_courant = take(east, jnp.full((SUB, lanes), 0, jnp.int32) + (base + 2 * depth + 1))
        depart = lane - off - 1 + far * lanes
        in_low = depart < 0
        index = depart & (lanes - 1)
        east_index = (lanes - 1 - east_off + far * lanes) & (lanes - 1)
        for t in range(depth):
            own = buf[0, t, span, :]
            near = buf[far, t, span, :]
            low = lo_buf[t, span, :]
            order = group * depth + t
            beyond = take(got_far[order // slots], (lane + RIM * (lax.rem(order, slots) + 1)) & (lanes - 1))
            ahead = take(east, (lane + (base + 2 * t)) & (lanes - 1))
            ahead = jnp.where(far == 1, own, ahead)
            near_left, near_right = edge_pair(near, low, ahead, lane)
            far_left, far_right = edge_pair(low, beyond, near, lane)
            near_prefix = prefix[far, t, span, :]
            far_total = jnp.where(far == 1, total[far, t, span, :], 0.0)

            def pick(near_table, low_table):
                return jnp.where(in_low, take(low_table, index), take(near_table, index))

            flux = (
                (prefix[0, t, span, :] - own + far_total)
                - pick(near_prefix, suffix[t, span, :])
                + frac_flux(courant, pick(near_right, far_right), pick(near_left, far_left), pick(near, low))
            )
            east_flux = (
                (total[0, t, span, :] + far_total)
                - take(near_prefix, east_index)
                + frac_flux(
                    east_courant, take(near_right, east_index), take(near_left, east_index), take(near, east_index)
                )
            )
            finish(t, first, own, flux, east_flux)

    edge_one = jnp.where(south_end, groups - 1, 0)
    edge_two = jnp.where(north_end, 1, jnp.where(south_end, groups - 2, groups - 1))
    to_south = remote(after.at[:, pl.ds(SUB, SUB)], after.at[:, pl.ds(SUB + rows, SUB)], 6, lat_dev(-1))
    to_north = remote(after.at[:, pl.ds(rows, SUB)], after.at[:, pl.ds(0, SUB)], 7, lat_dev(1))
    inner = jnp.where(south_end, FULL_GROUPS, jnp.where(north_end, 2, 1))
    pairs = jnp.where(polar, (groups - FULL_GROUPS) // 2 - 1, groups // 2 - 1)

    def pair(i, carry):
        pl.when(i == 1)(arrive)
        pl.when(i == 2)(arrive_rest)
        near_zonal(jnp.where(i < 2, edge_one, inner + 2 * i - 4))
        near_zonal(jnp.where(i < 2, edge_two, inner + 2 * i - 3))

        @pl.when(i == 1)
        def _():
            pl.when(has_south)(to_south.start)
            pl.when(has_north)(to_north.start)

        return carry

    lax.fori_loop(0, pairs + 2, pair, 0)

    @pl.when(polar)
    def _():
        for copy in polar_copies:
            copy.wait()
        lo_buf[:, full_span, :] = buf[1, :, full_span, :]
        lo_buf[:, polar_span, :] = west_two[:, polar_span, :]
        for t in range(depth):
            both = split_dot(buf[1, t, polar_span, :], prefix_matrix)
            prefix[1, t, polar_span, :] = both[:, :lanes]
            total[1, t, polar_span, :] = both[:, lanes:]
            suffix[t, full_span, :] = split_dot(lo_buf[t, full_span, :], suffix_matrix)

        def full_pair(i, carry):
            full_zonal(full_row // SUB + 2 * i)
            full_zonal(full_row // SUB + 2 * i + 1)
            return carry

        lax.fori_loop(0, FULL_GROUPS // 2, full_pair, 0)

    def merid(t, first, count):
        at = first + SUB
        edge_buf[t, at - 1 : at + count + 1, :] = wide_weight * (
            after[t, at - 2 : at + count, :] + after[t, at - 1 : at + count + 1, :]
        ) - narrow_weight * (after[t, at - 3 : at + count - 1, :] + after[t, at : at + count + 2, :])
        flux_buf[t, first : first + count + 1, :] = frac_flux(
            cn_buf[first : first + count + 1, :],
            edge_buf[t, at : at + count + 1, :],
            edge_buf[t, at - 1 : at + count, :],
            after[t, at - 1 : at + count, :],
        )
        done[t, first : first + count, :] = after[t, at : at + count, :] - (
            flux_buf[t, first + 1 : first + count + 1, :] - flux_buf[t, first : first + count, :]
        )

    def merid_inner(t, carry):
        merid(t, SUB, rows - 2 * SUB)
        return carry

    lax.fori_loop(0, depth, merid_inner, 0)

    @pl.when(has_south)
    def _():
        courant_copy.wait_send()
        to_south.wait_send()
        to_north.wait_recv()

    @pl.when(has_north)
    def _():
        to_north.wait_send()
        to_south.wait_recv()
        courant_copy.wait_recv()

    @pl.when(south_end)
    def _():
        after[:, 0:SUB, :] = jnp.zeros((depth, SUB, lanes), jnp.float32)
        cn_buf[0:1, :] = jnp.zeros((1, lanes), jnp.float32)

    @pl.when(north_end)
    def _():
        after[:, SUB + rows :, :] = jnp.zeros((depth, SUB, lanes), jnp.float32)
        cn_buf[rows:, :] = jnp.zeros((SUB, lanes), jnp.float32)

    def merid_rim(t, carry):
        merid(t, 0, SUB)
        merid(t, rows - SUB, SUB)
        return carry

    lax.fori_loop(0, depth, merid_rim, 0)


def store_kernel(done, out, sem):
    copies = [pltpu.make_async_copy(done.at[t], out.at[t], sem.at[t]) for t in range(out.shape[0])]
    for copy in copies:
        copy.start()
    for copy in copies:
        copy.wait()


def on_device(sizes, tracers, offsets, fraction, courant_north):
    tracer_count, level_count, rows, lanes = tracers.shape
    depth = tracer_count * level_count
    f32 = jnp.float32
    groups = rows // SUB
    slots = lanes // RIM
    tiles = -(-(depth * groups) // slots)
    column_tiles = -(-groups // slots)
    anywhere = pl.BlockSpec(memory_space=pl.ANY)
    vmem = pl.BlockSpec(memory_space=pltpu.VMEM)
    packed = pltpu.VMEM((tiles, SUB, lanes), f32)
    columns = pltpu.VMEM((column_tiles, SUB, lanes), f32)
    block = pltpu.VMEM((depth, rows, lanes), f32)
    two_blocks = pltpu.VMEM((2, depth, rows, lanes), f32)
    done = pl.pallas_call(
        functools.partial(step_kernel, sizes),
        out_shape=pltpu.VMEM((depth, rows, lanes), f32),
        in_specs=[pl.BlockSpec(memory_space=pltpu.HBM)] * 4,
        out_specs=vmem,
        scratch_shapes=[
            pltpu.VMEM((depth, rows + 2 * SUB, lanes), f32),
            pltpu.VMEM((rows + SUB, lanes), f32),
            pltpu.VMEM((depth, rows + 2 * SUB, lanes), f32),
            pltpu.VMEM((depth, rows + SUB, lanes), f32),
            two_blocks,
            pltpu.VMEM((rows, lanes), jnp.int32),
            pltpu.VMEM((rows, lanes), f32),
            block,
            packed, columns, packed, columns, packed,
            block, two_blocks, two_blocks, block,
            packed, packed, packed, packed, packed, packed, packed,
            pltpu.SemaphoreType.DMA((4,)),
            pltpu.SemaphoreType.DMA((10,)),
            pltpu.SemaphoreType.DMA((10,)),
        ],
        compiler_params=pltpu.CompilerParams(collective_id=0, has_side_effects=True, vmem_limit_bytes=66_747_392),
    )(tracers.reshape(depth, rows, lanes), offsets, fraction, courant_north)
    advected = pl.pallas_call(
        store_kernel,
        out_shape=jax.ShapeDtypeStruct((depth, rows, lanes), f32),
        in_specs=[vmem],
        out_specs=anywhere,
        scratch_shapes=[pltpu.SemaphoreType.DMA((depth,))],
        compiler_params=pltpu.CompilerParams(vmem_limit_bytes=8 << 20),
    )(done)
    return advected.reshape(tracers.shape)


def solution(mesh):
    placed = (P(None, None, "lat", "lon"), P("lat", "lon"), P("lat", "lon"), P("lat", "lon"))
    return jax.shard_map(
        functools.partial(on_device, (mesh.shape["lat"], mesh.shape["lon"])),
        mesh=mesh,
        in_specs=placed,
        out_specs=P(None, None, "lat", "lon"),
        check_vma=False,
    )
```
